32 devices in a mesh: groups: 2 (over x), band: 8 (over z, y), sub: 2 (over core).
Axes of the slice: x: 2, y: 2, z: 4, core: 2. Of those that a mesh axis runs over, the one named last changes fastest.
Arguments:
- sky_maps: bfloat16 [32, 2, 32, 16384], P(('groups', 'band', 'sub')), parts along dimension 0, may hold values from -6 to 6
- sky_mask: float32 [32, 16384], P(('groups', 'band', 'sub')), parts along dimension 0, may hold values from 0.005 to 1, as said below
- pixel_counts: int32 [32], P(('groups', 'band', 'sub')), parts along dimension 0, may hold values from 8192 to 16384, as said below
- phi_offsets: int32 [32], P(('groups', 'band', 'sub')), parts along dimension 0, may hold values from 0 to 1
- low_orders: int32 [32], P('groups'), parts along dimension 0, may hold values from 1 to 4095, as said below
- legendre: bfloat16 [32, 8192, 32], P(('groups', 'band', 'sub')), parts along dimension 0, may hold values from -1 to 1
Outputs:
- alm_packed: float32 [32, 8192, 128], P(('groups', 'band', 'sub')), parts along dimension 0
- spectra: float32 [16384, 2, 1024], P(('groups', 'band', 'sub')), parts along dimension 0
The draws below stay inside these ranges and needn't reach their ends.
There are 2 independent parts, one for each index of `groups`. The reference program is written for one: setup_inputs(seed, part) draws one part's arguments, and reference() takes and returns one part's arrays. A program takes and returns all parts, laid end to end along the dimension named above; each array names one. Nothing has to cross between parts.
Inputs may be any that keep to these rules, and one draw needn't show every extreme that they name: `pixel_counts`: multiples of 4; some cycle has exactly 16384 pixels; pixel slots at or past a cycle's count are not used. `low_orders`: all distinct. `sky_mask`: Positive.
All inputs are finite; a program needn't handle non-finite values.
Results may differ from the reference program's by a relative error of at most 0.0046.
Values may be sent and summed in bfloat16 or wider, within the bound.
A program may use at most 128 MiB of HBM per device.

```python
import math
import jax
import jax.numpy as jnp
from jax import lax

LMAX = 8192
PIXMAX = 16384
MAPS = 32
CYCLES = 16
PAIRS = 16


def draw_pixel_counts(key, part):
    quarters = jax.random.randint(key, (CYCLES,), PIXMAX // 8, PIXMAX // 4 + 1)
    counts = 4 * quarters
    longest = jax.random.randint(jax.random.fold_in(key, 7), (), 0, CYCLES)
    counts = jnp.where(jnp.arange(CYCLES) == longest, PIXMAX, counts)
    return counts.astype(jnp.int32)


def draw_low_orders(key, part):
    shuffled = jax.random.permutation(key, LMAX // 2 - 1)
    return (shuffled[:PAIRS] + 1).astype(jnp.int32)


def draw_sky_mask(key, part):
    position = jnp.arange(CYCLES, dtype=jnp.float32) / max(CYCLES - 1, 1)
    cycle_level = 10.0 ** (-0.5 + 0.5 * position)
    pixel_noise = jax.random.uniform(key, (CYCLES, PIXMAX), jnp.float32, 0.3, 1.0)
    return (cycle_level[:, None] * pixel_noise).astype(jnp.float32)


def set_ends(result, rng, smallest, largest):
    dims = result.shape
    place = [jax.random.randint(jax.random.fold_in(rng, axis), (), 0, dims[axis]) for axis in range(len(dims))]
    result = result.at[tuple(place)].set(smallest)
    longest = dims.index(max(dims))
    place[longest] = (place[longest] + 1) % dims[longest]
    return result.at[tuple(place)].set(largest)


def level_of(own_key, shape, pieces, low, top_value):
    gain = 1.0
    for dim, parts in pieces:
        draws = jax.random.uniform(jax.random.fold_in(jax.random.fold_in(own_key, 6), dim), (parts,), jnp.float32, low / len(pieces), top_value / len(pieces))
        gain = gain * jnp.repeat(jnp.exp(draws), shape[dim] // parts).reshape((-1,) + (1,) * (len(shape) - 1 - dim))
    return gain


def gaussian(key, shape, spread, most, pieces=(), kind=jnp.bfloat16):
    values = jax.random.normal(key, shape, jnp.float32) * spread
    if len(pieces) > 0:
        values = level_of(key, shape, pieces, -0.22, 0.18) * values
    return jnp.clip(values, min=-most, max=most).astype(kind)


def setup_inputs(seed: int = 0, part: int = 0) -> dict:
    key_of = jax.random.split(jax.random.key(seed), 7)
    part_keys = jax.random.split(jax.random.fold_in(key_of[6], part), 7)
    sky_maps = gaussian(part_keys[0], (CYCLES, 2, MAPS, PIXMAX), 1.0, 6.0, ((0, 16),))
    sky_mask = draw_sky_mask(jax.random.fold_in(jax.random.fold_in(key_of[6], part), 71), part)
    pixel_counts = draw_pixel_counts(jax.random.fold_in(jax.random.fold_in(key_of[6], part), 71), part)
    phi_offsets = set_ends(jax.random.randint(part_keys[3], (CYCLES,), 0, 2), jax.random.fold_in(part_keys[3], 1), 0, 1).astype(jnp.int32)
    low_orders = draw_low_orders(jax.random.fold_in(jax.random.fold_in(key_of[6], part), 71), part)
    legendre = gaussian(part_keys[5], (PAIRS, LMAX, 2 * CYCLES), (2 * CYCLES) ** -0.5, 1.0, ((0, 16),))
    return dict(sky_maps=sky_maps, sky_mask=sky_mask, pixel_counts=pixel_counts, phi_offsets=phi_offsets, low_orders=low_orders, legendre=legendre)


def slot_orders(low_orders):
    return jnp.stack([low_orders, LMAX - low_orders], axis=1).reshape(-1)

def finish_cycle(pixel_sums, cycle_count, orders):
    slots = orders.shape[0]
    maps_count = pixel_sums.shape[1] // 2
    inverse_root = 1.0 / jnp.sqrt(cycle_count.astype(jnp.float32))
    real_part = (pixel_sums[:slots] * inverse_root).reshape(slots, 2, maps_count)
    imag_part = (-pixel_sums[slots:] * inverse_root).reshape(slots, 2, maps_count)
    joined = jnp.stack([real_part[:, 0], imag_part[:, 0], real_part[:, 1], imag_part[:, 1]], axis=1).reshape(slots, 4 * maps_count)
    live_slots = 2 * orders < cycle_count
    return jnp.where(live_slots[:, None], joined, 0.0).astype(jnp.bfloat16)

def cycle_fourier(cycle_maps, cycle_mask, cycle_count, cycle_offset, orders):
    pixels = jnp.arange(PIXMAX, dtype=jnp.int32)
    cycle_rows = cycle_maps.reshape(2 * MAPS, PIXMAX).astype(jnp.float32)
    masked = jnp.where(pixels[None, :] < cycle_count, cycle_mask[None, :] * cycle_rows, 0.0).astype(jnp.bfloat16)
    phase_units = (2 * orders[:, None] * pixels[None, :] + orders[:, None] * cycle_offset) % (2 * cycle_count)
    phase_angle = jnp.pi * phase_units.astype(jnp.float32) / cycle_count.astype(jnp.float32)
    tables = jnp.concatenate([jnp.cos(phase_angle).astype(jnp.bfloat16), jnp.sin(phase_angle).astype(jnp.bfloat16)], axis=0)
    pixel_sums = jnp.dot(tables, masked.T, preferred_element_type=jnp.float32)
    return finish_cycle(pixel_sums, cycle_count, orders)

def stacked_operand(block_rows):
    quarter = block_rows.shape[1] // 4
    q_real = block_rows[:, :quarter]
    q_imag = block_rows[:, quarter:2 * quarter]
    u_real = block_rows[:, 2 * quarter:3 * quarter]
    u_imag = block_rows[:, 3 * quarter:]
    lower_half = jnp.concatenate([u_imag, -u_real, -q_imag, q_real], axis=1)
    return jnp.concatenate([block_rows, lower_half], axis=0)

def pair_alm(legendre_rows, first_order, first_block, second_block):
    both_operands = jnp.concatenate([stacked_operand(first_block), stacked_operand(second_block)], axis=1)
    product = -jnp.dot(legendre_rows, both_operands, preferred_element_type=jnp.float32)
    columns = first_block.shape[1]
    degree_count = legendre_rows.shape[0]
    degrees = jnp.arange(degree_count, dtype=jnp.int32)
    alm_rows = jnp.where((degrees < degree_count - first_order)[:, None], product[:, :columns], product[:, columns:])
    first_dense = jnp.where((degrees >= first_order)[:, None], jnp.roll(alm_rows, first_order, axis=0), 0.0).astype(jnp.bfloat16)
    second_dense = jnp.where((degrees >= degree_count - first_order)[:, None], alm_rows, 0.0).astype(jnp.bfloat16)
    return (alm_rows, jnp.stack([first_dense, second_dense], axis=0))

def reference(sky_maps, sky_mask, pixel_counts, phi_offsets, low_orders, legendre):
    orders = slot_orders(low_orders)

    def one_cycle(items):
        return cycle_fourier(items[0], items[1], items[2], items[3], orders)
    coefficients = lax.map(one_cycle, (sky_maps, sky_mask, pixel_counts, phi_offsets))
    by_slot = jnp.transpose(coefficients, (1, 0, 2)).reshape(PAIRS, 2, CYCLES, 4 * MAPS)

    def one_pair(items):
        return pair_alm(items[0], items[1], items[2][0], items[2][1])
    alm_packed, dense_pairs = lax.map(one_pair, (legendre, low_orders, by_slot))
    dense_rows = dense_pairs.reshape(2 * PAIRS, LMAX, 4 * MAPS)
    valid_pixels = jnp.arange(PIXMAX, dtype=jnp.int32)[None, :] < pixel_counts[:, None]
    weight = jnp.sum(jnp.where(valid_pixels, sky_mask * sky_mask, 0.0)) / jnp.sum(pixel_counts.astype(jnp.float32))
    block_rows = math.gcd(LMAX, 512)

    def spectra_block(first_degree):
        part_rows = lax.dynamic_slice_in_dim(dense_rows, first_degree, block_rows, 1).astype(jnp.float32)
        part_rows = part_rows.reshape(2 * PAIRS, block_rows, 2, 2, MAPS)
        totals = jnp.einsum('slerm,slern->lemn', part_rows, part_rows)
        degrees = first_degree + jnp.arange(block_rows, dtype=jnp.int32)
        counts = jnp.maximum(lax.optimization_barrier(jnp.sum((orders[None, :] <= degrees[:, None]).astype(jnp.int32), axis=1)), 1).astype(jnp.float32)
        return (2.0 * totals / (weight * counts)[:, None, None, None]).reshape(block_rows, 2, MAPS * MAPS)
    firsts = jnp.arange(LMAX // block_rows, dtype=jnp.int32) * block_rows
    spectra = lax.map(spectra_block, firsts).reshape(LMAX, 2, MAPS * MAPS)
    return (alm_packed, spectra)
```

```python
import functools

import jax
import jax.numpy as jnp
from jax import lax
from jax.experimental import pallas as pl
from jax.experimental.pallas import tpu as pltpu
from jax.sharding import PartitionSpec as P


def slot_orders(low_orders, degree_count):
    return jnp.stack([low_orders, degree_count - low_orders], axis=1).reshape(-1)


def finish_cycle(pixel_sums, cycle_count, orders):
    slots = orders.shape[0]
    maps_count = pixel_sums.shape[1] // 2
    inverse_root = 1.0 / jnp.sqrt(cycle_count.astype(jnp.float32))
    real_part = (pixel_sums[:slots] * inverse_root).reshape(slots, 2, maps_count)
    imag_part = (-pixel_sums[slots:] * inverse_root).reshape(slots, 2, maps_count)
    joined = jnp.stack(
        [real_part[:, 0], imag_part[:, 0], real_part[:, 1], imag_part[:, 1]], axis=1
    ).reshape(slots, 4 * maps_count)
    live_slots = 2 * orders < cycle_count
    return jnp.where(live_slots[:, None], joined, 0.0).astype(jnp.bfloat16)


def cycle_fourier(cycle_maps, cycle_mask, cycle_count, cycle_offset, orders):
    maps_count = cycle_maps.shape[1]
    pixel_slots = cycle_maps.shape[2]
    cycle_rows = cycle_maps.reshape(2 * maps_count, pixel_slots)
    block_width = min(2048, pixel_slots)
    group_count = block_width // 128
    slots = orders.shape[0]
    modulus = 2 * cycle_count
    scale = jnp.pi / cycle_count.astype(jnp.float32)
    order_mod = orders % modulus
    fine_units = 2 * order_mod[:, None] * jnp.arange(128, dtype=jnp.int32)[None, :] % modulus
    fine_angle = scale * fine_units.astype(jnp.float32)
    fine_cos = jnp.cos(fine_angle)[:, None, :]
    fine_sin = jnp.sin(fine_angle)[:, None, :]

    def add_block(block_index, totals):
        first_pixel = block_index * block_width
        row_block = lax.dynamic_slice_in_dim(cycle_rows, first_pixel, block_width, 1)
        mask_block = lax.dynamic_slice_in_dim(cycle_mask, first_pixel, block_width, 0)
        pixels = first_pixel + jnp.arange(block_width, dtype=jnp.int32)
        masked = jnp.where(
            pixels[None, :] < cycle_count, mask_block[None, :] * row_block.astype(jnp.float32), 0.0
        ).astype(jnp.bfloat16)
        group_starts = first_pixel + 128 * jnp.arange(group_count, dtype=jnp.int32)
        coarse_units = (
            order_mod[:, None] * ((2 * group_starts[None, :] + cycle_offset) % modulus) % modulus
        )
        coarse_angle = scale * coarse_units.astype(jnp.float32)
        coarse_cos = jnp.cos(coarse_angle)[:, :, None]
        coarse_sin = jnp.sin(coarse_angle)[:, :, None]
        cosines = (coarse_cos * fine_cos - coarse_sin * fine_sin).reshape(slots, block_width)
        sines = (coarse_sin * fine_cos + coarse_cos * fine_sin).reshape(slots, block_width)
        tables = jnp.concatenate([cosines.astype(jnp.bfloat16), sines.astype(jnp.bfloat16)], axis=0)
        return totals + lax.dot_general(
            tables, masked, (((1,), (1,)), ((), ())), preferred_element_type=jnp.float32
        )

    block_count = (cycle_count + block_width - 1) // block_width
    pixel_sums = lax.fori_loop(
        0, block_count, add_block, jnp.zeros((2 * slots, 2 * maps_count), jnp.float32)
    )
    return finish_cycle(pixel_sums, cycle_count, orders)


def stacked_operand(block_rows):
    quarter = block_rows.shape[1] // 4
    q_real = block_rows[:, :quarter]
    q_imag = block_rows[:, quarter : 2 * quarter]
    u_real = block_rows[:, 2 * quarter : 3 * quarter]
    u_imag = block_rows[:, 3 * quarter :]
    lower_half = jnp.concatenate([u_imag, -u_real, -q_imag, q_real], axis=1)
    return jnp.concatenate([block_rows, lower_half], axis=0)


def pair_alm(legendre_rows, first_order, first_block, second_block):
    first_operand = stacked_operand(first_block)
    second_operand = stacked_operand(second_block)
    degree_count, inner_width = legendre_rows.shape
    tile_height = min(128, degree_count)
    tile_count = degree_count // tile_height
    split_row = degree_count - first_order
    tile_starts = jnp.arange(tile_count, dtype=jnp.int32) * tile_height
    chosen = jnp.where(
        (tile_starts < split_row)[:, None, None], first_operand[None], second_operand[None]
    )
    tile_product = jnp.einsum(
        "tir,tro->tio",
        legendre_rows.reshape(tile_count, tile_height, inner_width),
        chosen,
        preferred_element_type=jnp.float32,
    )
    tile_product = tile_product.reshape(degree_count, first_operand.shape[1])
    border = split_row // tile_height * tile_height
    border_rows = lax.dynamic_slice_in_dim(legendre_rows, border, tile_height, 0)
    border_product = jnp.dot(border_rows, second_operand, preferred_element_type=jnp.float32)
    current = lax.dynamic_slice_in_dim(tile_product, border, tile_height, 0)
    row_index = border + jnp.arange(tile_height, dtype=jnp.int32)
    patched = jnp.where((row_index >= split_row)[:, None], border_product, current)
    return -lax.dynamic_update_slice_in_dim(tile_product, patched, border, 0)


def dense_pair(alm_rows, first_order):
    degree_count = alm_rows.shape[0]
    degrees = jnp.arange(degree_count, dtype=jnp.int32)
    first_dense = jnp.where(
        (degrees >= first_order)[:, None], jnp.roll(alm_rows, first_order, axis=0), 0.0
    ).astype(jnp.bfloat16)
    second_dense = jnp.where(
        (degrees >= degree_count - first_order)[:, None], alm_rows, 0.0
    ).astype(jnp.bfloat16)
    return jnp.stack([first_dense, second_dense], axis=0)


def outer_totals(rows, maps_count):
    split_parts = rows.reshape(rows.shape[0], rows.shape[1], 2, 2, maps_count)
    return jnp.einsum(
        "slerm,slern->lemn", split_parts, split_parts, preferred_element_type=jnp.float32
    )


def scaled_spectra(totals, degrees, orders, weight, maps_count):
    counts = jnp.maximum(
        jnp.sum((orders[None, :] <= degrees[:, None]).astype(jnp.int32), axis=1), 1
    ).astype(jnp.float32)
    return (2.0 * totals / (weight * counts)[:, None, None, None]).reshape(
        degrees.shape[0], 2, maps_count * maps_count
    )


EXTRA = 16


def fourier_kernel(maps_ref, mask_ref, fine_ref, coarse_ref, live_ref, out_ref, total):
    step = pl.program_id(0)
    slots = fine_ref.shape[1]
    groups = maps_ref.shape[1] // 128
    fine_cos = fine_ref[0]
    fine_sin = fine_ref[1]
    cosines = []
    sines = []
    for group in range(groups):
        coarse_cos = coarse_ref[0, 0, :, group : group + 1]
        coarse_sin = coarse_ref[1, 0, :, group : group + 1]
        cosines.append((coarse_cos * fine_cos - coarse_sin * fine_sin).astype(jnp.bfloat16))
        sines.append((coarse_sin * fine_cos + coarse_cos * fine_sin).astype(jnp.bfloat16))
    tables = jnp.concatenate(
        [jnp.concatenate(cosines, axis=1), jnp.concatenate(sines, axis=1)], axis=0
    )
    masked = (maps_ref[...].astype(jnp.float32) * mask_ref[...]).astype(jnp.bfloat16)
    sums = lax.dot_general(
        tables, masked, (((1,), (1,)), ((), ())), preferred_element_type=jnp.float32
    )

    @pl.when(step == 0)
    def _():
        total[...] = sums

    @pl.when(step > 0)
    def _():
        total[...] += sums

    @pl.when(step == pl.num_programs(0) - 1)
    def _():
        half = maps_ref.shape[0] // 2
        real = total[:slots]
        imag = -total[slots:]
        joined = jnp.concatenate(
            [real[:, :half], imag[:, :half], real[:, half:], imag[:, half:]], axis=1
        )
        out_ref[...] = (joined * live_ref[...]).astype(jnp.bfloat16)


def fourier_call(cycle_maps, masked_weight, cycle_count, cycle_offset, orders):
    maps_count = cycle_maps.shape[1]
    pixel_slots = cycle_maps.shape[2]
    rows = cycle_maps.reshape(2 * maps_count, pixel_slots)
    slots = orders.shape[0]
    width = min(2048, pixel_slots)
    blocks = pixel_slots // width
    groups = width // 128
    modulus = 2 * cycle_count
    scale = jnp.pi / cycle_count.astype(jnp.float32)
    order_mod = orders % modulus
    fine_units = 2 * order_mod[:, None] * jnp.arange(128, dtype=jnp.int32)[None, :] % modulus
    starts = 128 * jnp.arange(blocks * groups, dtype=jnp.int32)
    starts = ((2 * starts + cycle_offset) % modulus).reshape(blocks, 1, groups)
    coarse_units = order_mod[None, :, None] * starts % modulus
    fine_angle = scale * fine_units.astype(jnp.float32)
    coarse_angle = scale * coarse_units.astype(jnp.float32)
    fine = jnp.stack([jnp.cos(fine_angle), jnp.sin(fine_angle)])
    coarse = jnp.stack([jnp.cos(coarse_angle), jnp.sin(coarse_angle)])
    inverse_root = 1.0 / jnp.sqrt(cycle_count.astype(jnp.float32))
    live = jnp.broadcast_to(
        jnp.where(2 * orders < cycle_count, inverse_root, 0.0)[:, None], (slots, 4 * maps_count)
    )
    return pl.pallas_call(
        fourier_kernel,
        grid=(blocks,),
        in_specs=[
            pl.BlockSpec((2 * maps_count, width), lambda i: (0, i)),
            pl.BlockSpec((1, width), lambda i: (0, i)),
            pl.BlockSpec((2, slots, 128), lambda i: (0, 0, 0)),
            pl.BlockSpec((2, 1, slots, groups), lambda i: (0, i, 0, 0)),
            pl.BlockSpec((slots, 4 * maps_count), lambda i: (0, 0)),
        ],
        out_specs=pl.BlockSpec((slots, 4 * maps_count), lambda i: (0, 0)),
        out_shape=jax.ShapeDtypeStruct((slots, 4 * maps_count), jnp.bfloat16),
        scratch_shapes=[pltpu.VMEM((2 * slots, 2 * maps_count), jnp.float32)],
        cost_estimate=pl.CostEstimate(
            flops=8 * slots * maps_count * pixel_slots,
            bytes_accessed=4 * maps_count * pixel_slots,
            transcendentals=0,
        ),
    )(rows, masked_weight, fine, coarse, live)


def operand_rows(wide, slot, cycles, stride):
    upper = wide[pl.ds(slot, cycles, stride=stride), :]
    quarter = upper.shape[1] // 4
    lower = jnp.concatenate(
        [
            upper[:, 3 * quarter :],
            -upper[:, 2 * quarter : 3 * quarter],
            -upper[:, quarter : 2 * quarter],
            upper[:, :quarter],
        ],
        axis=1,
    )
    return jnp.concatenate([upper, lower], axis=0)


def alm_kernel(stride, scalar_ref, gathered_ref, legendre_ref, out_ref, wide, operand):
    step = pl.program_id(0)
    height = out_ref.shape[0]
    columns = out_ref.shape[1]
    cycles = gathered_ref.shape[0] // stride

    @pl.when(step == 0)
    def _():
        wide[...] = gathered_ref[...].astype(jnp.float32)
        pair = scalar_ref[0]
        operand[...] = -jnp.concatenate(
            [
                operand_rows(wide, 2 * pair, cycles, stride),
                operand_rows(wide, 2 * pair + 1, cycles, stride),
            ],
            axis=1,
        )

    product = lax.dot_general(
        legendre_ref[...],
        operand[...].astype(jnp.bfloat16),
        (((0,), (0,)), ((), ())),
        preferred_element_type=jnp.float32,
    )
    row = step * height + lax.broadcasted_iota(jnp.int32, (height, columns), 0)
    out_ref[...] = jnp.where(row < scalar_ref[1], product[:, :columns], product[:, columns:])


def alm_call(scalars, gathered, stride, legendre_cols):
    inner, degree_count = legendre_cols.shape
    columns = gathered.shape[1]
    height = min(1024, degree_count)
    return pl.pallas_call(
        functools.partial(alm_kernel, stride),
        grid=(degree_count // height,),
        in_specs=[
            pl.BlockSpec(memory_space=pltpu.SMEM),
            pl.BlockSpec(gathered.shape, lambda i: (0, 0)),
            pl.BlockSpec((inner, height), lambda i: (0, i)),
        ],
        out_specs=pl.BlockSpec((height, columns), lambda i: (i, 0)),
        out_shape=jax.ShapeDtypeStruct((degree_count, columns), jnp.float32),
        scratch_shapes=[
            pltpu.VMEM(gathered.shape, jnp.float32),
            pltpu.VMEM((inner, 2 * columns), jnp.float32),
        ],
        cost_estimate=pl.CostEstimate(
            flops=4 * degree_count * inner * columns,
            bytes_accessed=4 * degree_count * columns,
            transcendentals=0,
        ),
    )(scalars, gathered, legendre_cols)


def spectra_kernel(stride, scale_ref, gathered_ref, legendre_ref, out_ref, wide, operands, dense, turned):
    step = pl.program_id(0)
    cycles = gathered_ref.shape[0] // stride
    inner = 2 * cycles
    slots = legendre_ref.shape[0] // inner
    height = legendre_ref.shape[1]
    per_group = 128 // inner
    group_count = slots // per_group

    @pl.when(step == 0)
    def _():
        wide[...] = gathered_ref[...].astype(jnp.float32)
        for slot in range(slots):
            operands[slot * inner : (slot + 1) * inner, :] = operand_rows(
                wide, slot, cycles, stride
            ).astype(jnp.bfloat16)

    def spread(tall, piece):
        parts = []
        for index in range(128 // piece):
            own = tall[index * piece : (index + 1) * piece]
            column = []
            if index > 0:
                column.append(jnp.zeros((index * piece, 128), tall.dtype))
            column.append(own)
            if (index + 1) * piece < 128:
                column.append(jnp.zeros((128 - (index + 1) * piece, 128), tall.dtype))
            parts.append(jnp.concatenate(column, axis=0))
        return jnp.concatenate(parts, axis=1)

    for group in range(group_count):
        wide_operand = spread(operands[group * 128 : (group + 1) * 128, :], inner)
        product = lax.dot_general(
            legendre_ref[group * 128 : (group + 1) * 128, :],
            wide_operand,
            (((0,), (0,)), ((), ())),
            preferred_element_type=jnp.float32,
        )
        for index in range(per_group):
            dense[pl.ds(group * per_group + index, height, stride=slots), :] = product[
                :, index * 128 : (index + 1) * 128
            ]

    per_batch = 128 // slots
    lane_group = lax.broadcasted_iota(jnp.int32, (8, 128), 1) // 32

    def batch(position, carry):
        rows = dense[pl.ds(pl.multiple_of(position * 128, 128), 128), :]
        turned[...] = rows.T
        left = jnp.concatenate(
            [
                turned[pl.ds(32 * part + quarter, 8, stride=4), :]
                for part in range(4)
                for quarter in range(4)
            ],
            axis=0,
        ).astype(jnp.bfloat16)
        gram = jnp.dot(
            left, spread(rows.astype(jnp.bfloat16), slots), preferred_element_type=jnp.float32
        )
        for index in range(per_batch):
            degree = position * per_batch + index
            factor = scale_ref[step * height + degree]
            for kind in range(2):
                result = None
                for turn in range(4):
                    first = 32 * (2 * kind) + 8 * ((2 * kind + turn) % 4)
                    second = 32 * (2 * kind + 1) + 8 * ((2 * kind + 1 + turn) % 4)
                    lanes = slice(index * 128, (index + 1) * 128)
                    value = jnp.where(
                        lane_group == 2 * kind,
                        gram[first : first + 8, lanes],
                        jnp.where(
                            lane_group == 2 * kind + 1, gram[second : second + 8, lanes], 0.0
                        ),
                    )
                    if turn > 0:
                        value = pltpu.roll(value, 32 * turn, axis=1)
                    result = value if result is None else result + value
                out_ref[pl.ds(degree * 16 + kind, 8, stride=2), :] = result * factor
        return carry

    lax.fori_loop(0, height // per_batch, batch, 0, unroll=2)


def spectra_call(scale, gathered, stride, legendre_rows):
    row_count, degree_local = legendre_rows.shape
    columns = gathered.shape[1]
    inner = 2 * (gathered.shape[0] // stride)
    slots = row_count // inner
    height = 128
    result = pl.pallas_call(
        functools.partial(spectra_kernel, stride),
        grid=(degree_local // height,),
        in_specs=[
            pl.BlockSpec(memory_space=pltpu.SMEM),
            pl.BlockSpec(gathered.shape, lambda i: (0, 0)),
            pl.BlockSpec((row_count, height), lambda i: (0, i)),
        ],
        out_specs=pl.BlockSpec((height * 16, 128), lambda i: (i, 0)),
        out_shape=jax.ShapeDtypeStruct((degree_local * 16, 128), jnp.float32),
        scratch_shapes=[
            pltpu.VMEM(gathered.shape, jnp.float32),
            pltpu.VMEM((row_count, columns), jnp.bfloat16),
            pltpu.VMEM((height * slots, columns), jnp.float32),
            pltpu.VMEM((128, 128), jnp.float32),
        ],
        cost_estimate=pl.CostEstimate(
            flops=degree_local * slots * 4 * columns * columns,
            bytes_accessed=4 * degree_local * 2048,
            transcendentals=0,
        ),
    )(scale, gathered, legendre_rows)
    return (
        result.reshape(degree_local, 8, 2, 128)
        .transpose(0, 2, 1, 3)
        .reshape(degree_local, 2, 1024)
    )


def split_three(value):
    pieces = []
    rest = value
    for _ in range(3):
        piece = lax.reduce_precision(rest, 8, 7)
        pieces.append(piece)
        rest = rest - piece
    return pieces


def compact(sky_maps, sky_mask, pixel_counts, phi_offsets, low_orders, legendre):
    axes = ("band", "sub")
    devices = lax.axis_size(axes)
    device_index = lax.axis_index(axes)
    degree_count = legendre.shape[1]
    inner = legendre.shape[2]
    slots = 2 * low_orders.shape[0]
    orders = slot_orders(low_orders, degree_count)
    degree_local = degree_count // devices
    first_order = lax.dynamic_index_in_dim(low_orders, device_index, 0, keepdims=False)
    split_row = degree_count - first_order
    legendre_cols = legendre[0].T
    degrees = jnp.arange(degree_count, dtype=jnp.int32)[None, :]
    doubled = jnp.concatenate([legendre_cols, legendre_cols], axis=1)
    rolled = lax.dynamic_slice_in_dim(doubled, split_row, degree_count, 1)
    first = jnp.where(degrees >= first_order, rolled, 0.0).astype(jnp.bfloat16)
    second = jnp.where(degrees >= split_row, legendre_cols, 0.0).astype(jnp.bfloat16)
    sent = jnp.concatenate([first, second], axis=0)
    sent = sent.reshape(2 * inner, devices, degree_local).transpose(1, 0, 2)
    received = lax.all_to_all(sent, axes, split_axis=0, concat_axis=0, tiled=True)
    legendre_rows = received.reshape(slots * inner, degree_local)

    count = pixel_counts[0]
    valid = jnp.arange(sky_mask.shape[1], dtype=jnp.int32)[None, :] < count
    masked_weight = jnp.where(valid, sky_mask, 0.0)
    coefficients = fourier_call(sky_maps[0], masked_weight, count, phi_offsets[0], orders)
    square = split_three(jnp.sum(masked_weight * masked_weight))
    pixels = split_three(count.astype(jnp.float32))
    columns = coefficients.shape[1]
    extra = jnp.zeros((EXTRA, columns), jnp.float32)
    column_index = lax.broadcasted_iota(jnp.int32, (EXTRA, columns), 1)
    for index, piece in enumerate(square + pixels):
        extra = jnp.where(column_index == index, piece, extra)
    payload = jnp.concatenate([coefficients, extra.astype(jnp.bfloat16)], axis=0)
    gathered = lax.all_gather(payload, axes, axis=0, tiled=True)
    stride = slots + EXTRA
    pieces = gathered.reshape(devices, stride, columns)[:, slots, :6].astype(jnp.float32)
    weight = jnp.sum(pieces[:, :3]) / jnp.sum(pieces[:, 3:])
    scalars = jnp.stack([device_index.astype(jnp.int32), split_row])
    alm_packed = alm_call(scalars, gathered, stride, legendre_cols)
    own = device_index * degree_local + jnp.arange(degree_local, dtype=jnp.int32)
    counts = jnp.maximum(
        jnp.sum((orders[None, :] <= own[:, None]).astype(jnp.int32), axis=1), 1
    ).astype(jnp.float32)
    scale = 2.0 / (weight * counts)
    spectra = spectra_call(scale, gathered, stride, legendre_rows)
    return (alm_packed[None], spectra)


def general(sky_maps, sky_mask, pixel_counts, phi_offsets, low_orders, legendre):
    devices = lax.axis_size(("band", "sub"))
    device_index = lax.axis_index(("band", "sub"))
    degree_count = legendre.shape[1]
    orders = slot_orders(low_orders, degree_count)
    cycle_local = sky_maps.shape[0]
    maps_count = sky_maps.shape[2]
    pair_local = legendre.shape[0]
    slot_local = 2 * pair_local
    columns = 4 * maps_count
    valid_pixels = jnp.arange(sky_maps.shape[3], dtype=jnp.int32)[None, :] < pixel_counts[:, None]
    local_square = jnp.sum(jnp.where(valid_pixels, sky_mask * sky_mask, 0.0))
    local_pixels = jnp.sum(pixel_counts.astype(jnp.float32))
    total_square, total_pixels = lax.psum((local_square, local_pixels), ("band", "sub"))
    weight = total_square / total_pixels
    cycle_blocks = [
        cycle_fourier(sky_maps[0], sky_mask[0], pixel_counts[0], phi_offsets[0], orders)
    ]
    coefficients = jnp.stack(cycle_blocks, axis=1).reshape(
        devices, slot_local, cycle_local, columns
    )
    received = lax.all_to_all(
        coefficients, ("band", "sub"), split_axis=0, concat_axis=0, tiled=True
    )
    cycle_total = devices * cycle_local
    first_order = lax.dynamic_index_in_dim(
        low_orders, device_index * pair_local + 0, 0, keepdims=False
    )
    first_block = received[:, 0].reshape(cycle_total, columns)
    second_block = received[:, 1].reshape(cycle_total, columns)
    alm_pairs = [pair_alm(legendre[0], first_order, first_block, second_block)]
    alm_packed = jnp.stack(alm_pairs, axis=0)
    dense_local = dense_pair(alm_pairs[0], first_order)
    by_degree = lax.all_to_all(
        dense_local, ("band", "sub"), split_axis=1, concat_axis=0, tiled=True
    )
    degree_local = by_degree.shape[1]
    degrees = device_index * degree_local + jnp.arange(degree_local, dtype=jnp.int32)
    totals = outer_totals(by_degree, maps_count)
    spectra = scaled_spectra(totals, degrees, orders, weight, maps_count)
    return (alm_packed, spectra)


def local(sky_maps, sky_mask, pixel_counts, phi_offsets, low_orders, legendre):
    devices = lax.axis_size(("band", "sub"))
    fits = (
        sky_maps.shape[0] == 1
        and legendre.shape[0] == 1
        and sky_maps.shape[2] == 32
        and sky_maps.shape[3] % 2048 == 0
        and 2 * low_orders.shape[0] in (16, 32, 64)
        and legendre.shape[2] == 2 * devices
        and legendre.shape[2] in (16, 32, 64)
        and legendre.shape[1] % (128 * devices) == 0
        and legendre.shape[1] % 1024 == 0
    )
    body = compact if fits else general
    return body(sky_maps, sky_mask, pixel_counts, phi_offsets, low_orders, legendre)


def solution(mesh):
    placed = (
        P(("groups", "band", "sub"), None, None, None),
        P(("groups", "band", "sub"), None),
        P(("groups", "band", "sub")),
        P(("groups", "band", "sub")),
        P("groups"),
        P(("groups", "band", "sub"), None, None),
    )
    return jax.shard_map(
        local,
        mesh=mesh,
        in_specs=placed,
        out_specs=(
            P(("groups", "band", "sub"), None, None),
            P(("groups", "band", "sub"), None, None),
        ),
        check_vma=False,
    )
```

```python
import functools

import jax
import jax.numpy as jnp
from jax import lax
from jax.experimental import pallas as pl
from jax.experimental.pallas import tpu as pltpu
from jax.sharding import PartitionSpec as P


def slot_orders(low_orders, degree_count):
    return jnp.stack([low_orders, degree_count - low_orders], axis=1).reshape(-1)


def finish_cycle(pixel_sums, cycle_count, orders):
    slots = orders.shape[0]
    maps_count = pixel_sums.shape[1] // 2
    inverse_root = 1.0 / jnp.sqrt(cycle_count.astype(jnp.float32))
    real_part = (pixel_sums[:slots] * inverse_root).reshape(slots, 2, maps_count)
    imag_part = (-pixel_sums[slots:] * inverse_root).reshape(slots, 2, maps_count)
    joined = jnp.stack(
        [real_part[:, 0], imag_part[:, 0], real_part[:, 1], imag_part[:, 1]], axis=1
    ).reshape(slots, 4 * maps_count)
    live_slots = 2 * orders < cycle_count
    return jnp.where(live_slots[:, None], joined, 0.0).astype(jnp.bfloat16)


def cycle_fourier(cycle_maps, cycle_mask, cycle_count, cycle_offset, orders):
    maps_count = cycle_maps.shape[1]
    pixel_slots = cycle_maps.shape[2]
    cycle_rows = cycle_maps.reshape(2 * maps_count, pixel_slots)
    block_width = min(2048, pixel_slots)
    group_count = block_width // 128
    slots = orders.shape[0]
    modulus = 2 * cycle_count
    scale = jnp.pi / cycle_count.astype(jnp.float32)
    order_mod = orders % modulus
    fine_units = 2 * order_mod[:, None] * jnp.arange(128, dtype=jnp.int32)[None, :] % modulus
    fine_angle = scale * fine_units.astype(jnp.float32)
    fine_cos = jnp.cos(fine_angle)[:, None, :]
    fine_sin = jnp.sin(fine_angle)[:, None, :]

    def add_block(block_index, totals):
        first_pixel = block_index * block_width
        row_block = lax.dynamic_slice_in_dim(cycle_rows, first_pixel, block_width, 1)
        mask_block = lax.dynamic_slice_in_dim(cycle_mask, first_pixel, block_width, 0)
        pixels = first_pixel + jnp.arange(block_width, dtype=jnp.int32)
        masked = jnp.where(
            pixels[None, :] < cycle_count, mask_block[None, :] * row_block.astype(jnp.float32), 0.0
        ).astype(jnp.bfloat16)
        group_starts = first_pixel + 128 * jnp.arange(group_count, dtype=jnp.int32)
        coarse_units = (
            order_mod[:, None] * ((2 * group_starts[None, :] + cycle_offset) % modulus) % modulus
        )
        coarse_angle = scale * coarse_units.astype(jnp.float32)
        coarse_cos = jnp.cos(coarse_angle)[:, :, None]
        coarse_sin = jnp.sin(coarse_angle)[:, :, None]
        cosines = (coarse_cos * fine_cos - coarse_sin * fine_sin).reshape(slots, block_width)
        sines = (coarse_sin * fine_cos + coarse_cos * fine_sin).reshape(slots, block_width)
        tables = jnp.concatenate([cosines.astype(jnp.bfloat16), sines.astype(jnp.bfloat16)], axis=0)
        return totals + lax.dot_general(
            tables, masked, (((1,), (1,)), ((), ())), preferred_element_type=jnp.float32
        )

    block_count = (cycle_count + block_width - 1) // block_width
    pixel_sums = lax.fori_loop(
        0, block_count, add_block, jnp.zeros((2 * slots, 2 * maps_count), jnp.float32)
    )
    return finish_cycle(pixel_sums, cycle_count, orders)


def stacked_operand(block_rows):
    quarter = block_rows.shape[1] // 4
    q_real = block_rows[:, :quarter]
    q_imag = block_rows[:, quarter : 2 * quarter]
    u_real = block_rows[:, 2 * quarter : 3 * quarter]
    u_imag = block_rows[:, 3 * quarter :]
    lower_half = jnp.concatenate([u_imag, -u_real, -q_imag, q_real], axis=1)
    return jnp.concatenate([block_rows, lower_half], axis=0)


def pair_alm(legendre_rows, first_order, first_block, second_block):
    first_operand = stacked_operand(first_block)
    second_operand = stacked_operand(second_block)
    degree_count, inner_width = legendre_rows.shape
    tile_height = min(128, degree_count)
    tile_count = degree_count // tile_height
    split_row = degree_count - first_order
    tile_starts = jnp.arange(tile_count, dtype=jnp.int32) * tile_height
    chosen = jnp.where(
        (tile_starts < split_row)[:, None, None], first_operand[None], second_operand[None]
    )
    tile_product = jnp.einsum(
        "tir,tro->tio",
        legendre_rows.reshape(tile_count, tile_height, inner_width),
        chosen,
        preferred_element_type=jnp.float32,
    )
    tile_product = tile_product.reshape(degree_count, first_operand.shape[1])
    border = split_row // tile_height * tile_height
    border_rows = lax.dynamic_slice_in_dim(legendre_rows, border, tile_height, 0)
    border_product = jnp.dot(border_rows, second_operand, preferred_element_type=jnp.float32)
    current = lax.dynamic_slice_in_dim(tile_product, border, tile_height, 0)
    row_index = border + jnp.arange(tile_height, dtype=jnp.int32)
    patched = jnp.where((row_index >= split_row)[:, None], border_product, current)
    return -lax.dynamic_update_slice_in_dim(tile_product, patched, border, 0)


def dense_pair(alm_rows, first_order):
    degree_count = alm_rows.shape[0]
    degrees = jnp.arange(degree_count, dtype=jnp.int32)
    first_dense = jnp.where(
        (degrees >= first_order)[:, None], jnp.roll(alm_rows, first_order, axis=0), 0.0
    ).astype(jnp.bfloat16)
    second_dense = jnp.where(
        (degrees >= degree_count - first_order)[:, None], alm_rows, 0.0
    ).astype(jnp.bfloat16)
    return jnp.stack([first_dense, second_dense], axis=0)


def outer_totals(rows, maps_count):
    split_parts = rows.reshape(rows.shape[0], rows.shape[1], 2, 2, maps_count)
    return jnp.einsum(
        "slerm,slern->lemn", split_parts, split_parts, preferred_element_type=jnp.float32
    )


def scaled_spectra(totals, degrees, orders, weight, maps_count):
    counts = jnp.maximum(
        jnp.sum((orders[None, :] <= degrees[:, None]).astype(jnp.int32), axis=1), 1
    ).astype(jnp.float32)
    return (2.0 * totals / (weight * counts)[:, None, None, None]).reshape(
        degrees.shape[0], 2, maps_count * maps_count
    )


EXTRA = 16


def fourier_kernel(maps_ref, mask_ref, fine_ref, coarse_ref, live_ref, out_ref, total):
    step = pl.program_id(0)
    slots = fine_ref.shape[1]
    groups = maps_ref.shape[1] // 128
    fine_cos = fine_ref[0]
    fine_sin = fine_ref[1]
    cosines = []
    sines = []
    for group in range(groups):
        coarse_cos = coarse_ref[0, 0, :, group : group + 1]
        coarse_sin = coarse_ref[1, 0, :, group : group + 1]
        cosines.append((coarse_cos * fine_cos - coarse_sin * fine_sin).astype(jnp.bfloat16))
        sines.append((coarse_sin * fine_cos + coarse_cos * fine_sin).astype(jnp.bfloat16))
    tables = jnp.concatenate(
        [jnp.concatenate(cosines, axis=1), jnp.concatenate(sines, axis=1)], axis=0
    )
    masked = (maps_ref[...].astype(jnp.float32) * mask_ref[...]).astype(jnp.bfloat16)
    sums = lax.dot_general(
        tables, masked, (((1,), (1,)), ((), ())), preferred_element_type=jnp.float32
    )

    @pl.when(step == 0)
    def _():
        total[...] = sums

    @pl.when(step > 0)
    def _():
        total[...] += sums

    @pl.when(step == pl.num_programs(0) - 1)
    def _():
        half = maps_ref.shape[0] // 2
        real = total[:slots]
        imag = -total[slots:]
        joined = jnp.concatenate(
            [real[:, :half], imag[:, :half], real[:, half:], imag[:, half:]], axis=1
        )
        out_ref[...] = (joined * live_ref[...]).astype(jnp.bfloat16)


def fourier_call(cycle_maps, masked_weight, cycle_count, cycle_offset, orders):
    maps_count = cycle_maps.shape[1]
    pixel_slots = cycle_maps.shape[2]
    rows = cycle_maps.reshape(2 * maps_count, pixel_slots)
    slots = orders.shape[0]
    width = min(2048, pixel_slots)
    blocks = pixel_slots // width
    groups = width // 128
    modulus = 2 * cycle_count
    scale = jnp.pi / cycle_count.astype(jnp.float32)
    order_mod = orders % modulus
    fine_units = 2 * order_mod[:, None] * jnp.arange(128, dtype=jnp.int32)[None, :] % modulus
    starts = 128 * jnp.arange(blocks * groups, dtype=jnp.int32)
    starts = ((2 * starts + cycle_offset) % modulus).reshape(blocks, 1, groups)
    coarse_units = order_mod[None, :, None] * starts % modulus
    fine_angle = scale * fine_units.astype(jnp.float32)
    coarse_angle = scale * coarse_units.astype(jnp.float32)
    fine = jnp.stack([jnp.cos(fine_angle), jnp.sin(fine_angle)])
    coarse = jnp.stack([jnp.cos(coarse_angle), jnp.sin(coarse_angle)])
    inverse_root = 1.0 / jnp.sqrt(cycle_count.astype(jnp.float32))
    live = jnp.broadcast_to(
        jnp.where(2 * orders < cycle_count, inverse_root, 0.0)[:, None], (slots, 4 * maps_count)
    )
    return pl.pallas_call(
        fourier_kernel,
        grid=(blocks,),
        in_specs=[
            pl.BlockSpec((2 * maps_count, width), lambda i: (0, i)),
            pl.BlockSpec((1, width), lambda i: (0, i)),
            pl.BlockSpec((2, slots, 128), lambda i: (0, 0, 0)),
            pl.BlockSpec((2, 1, slots, groups), lambda i: (0, i, 0, 0)),
            pl.BlockSpec((slots, 4 * maps_count), lambda i: (0, 0)),
        ],
        out_specs=pl.BlockSpec((slots, 4 * maps_count), lambda i: (0, 0)),
        out_shape=jax.ShapeDtypeStruct((slots, 4 * maps_count), jnp.bfloat16),
        scratch_shapes=[pltpu.VMEM((2 * slots, 2 * maps_count), jnp.float32)],
        cost_estimate=pl.CostEstimate(
            flops=8 * slots * maps_count * pixel_slots,
            bytes_accessed=4 * maps_count * pixel_slots,
            transcendentals=0,
        ),
    )(rows, masked_weight, fine, coarse, live)


def operand_rows(wide, slot, cycles, stride):
    upper = wide[pl.ds(slot, cycles, stride=stride), :]
    quarter = upper.shape[1] // 4
    lower = jnp.concatenate(
        [
            upper[:, 3 * quarter :],
            -upper[:, 2 * quarter : 3 * quarter],
            -upper[:, quarter : 2 * quarter],
            upper[:, :quarter],
        ],
        axis=1,
    )
    return jnp.concatenate([upper, lower], axis=0)


def alm_kernel(stride, scalar_ref, gathered_ref, legendre_ref, out_ref, wide, operand):
    step = pl.program_id(0)
    height = out_ref.shape[0]
    columns = out_ref.shape[1]
    cycles = gathered_ref.shape[0] // stride

    @pl.when(step == 0)
    def _():
        wide[...] = gathered_ref[...].astype(jnp.float32)
        pair = scalar_ref[0]
        operand[...] = -jnp.concatenate(
            [
                operand_rows(wide, 2 * pair, cycles, stride),
                operand_rows(wide, 2 * pair + 1, cycles, stride),
            ],
            axis=1,
        )

    product = lax.dot_general(
        legendre_ref[...],
        operand[...].astype(jnp.bfloat16),
        (((0,), (0,)), ((), ())),
        preferred_element_type=jnp.float32,
    )
    row = step * height + lax.broadcasted_iota(jnp.int32, (height, columns), 0)
    out_ref[...] = jnp.where(row < scalar_ref[1], product[:, :columns], product[:, columns:])


def alm_call(scalars, gathered, stride, legendre_cols):
    inner, degree_count = legendre_cols.shape
    columns = gathered.shape[1]
    height = min(1024, degree_count)
    return pl.pallas_call(
        functools.partial(alm_kernel, stride),
        grid=(degree_count // height,),
        in_specs=[
            pl.BlockSpec(memory_space=pltpu.SMEM),
            pl.BlockSpec(gathered.shape, lambda i: (0, 0)),
            pl.BlockSpec((inner, height), lambda i: (0, i)),
        ],
        out_specs=pl.BlockSpec((height, columns), lambda i: (i, 0)),
        out_shape=jax.ShapeDtypeStruct((degree_count, columns), jnp.float32),
        scratch_shapes=[
            pltpu.VMEM(gathered.shape, jnp.float32),
            pltpu.VMEM((inner, 2 * columns), jnp.float32),
        ],
        cost_estimate=pl.CostEstimate(
            flops=4 * degree_count * inner * columns,
            bytes_accessed=4 * degree_count * columns,
            transcendentals=0,
        ),
    )(scalars, gathered, legendre_cols)


def spectra_kernel(stride, scale_ref, gathered_ref, legendre_ref, out_ref, wide, operands, dense, turned):
    step = pl.program_id(0)
    cycles = gathered_ref.shape[0] // stride
    inner = 2 * cycles
    slots = legendre_ref.shape[0] // inner
    height = legendre_ref.shape[1]
    per_group = 128 // inner
    group_count = slots // per_group

    @pl.when(step == 0)
    def _():
        wide[...] = gathered_ref[...].astype(jnp.float32)
        for slot in range(slots):
            operands[slot * inner : (slot + 1) * inner, :] = operand_rows(
                wide, slot, cycles, stride
            ).astype(jnp.bfloat16)

    def spread(tall, piece):
        parts = []
        for index in range(128 // piece):
            own = tall[index * piece : (index + 1) * piece]
            column = []
            if index > 0:
                column.append(jnp.zeros((index * piece, 128), tall.dtype))
            column.append(own)
            if (index + 1) * piece < 128:
                column.append(jnp.zeros((128 - (index + 1) * piece, 128), tall.dtype))
            parts.append(jnp.concatenate(column, axis=0))
        return jnp.concatenate(parts, axis=1)

    for group in range(group_count):
        wide_operand = spread(operands[group * 128 : (group + 1) * 128, :], inner)
        product = lax.dot_general(
            legendre_ref[group * 128 : (group + 1) * 128, :],
            wide_operand,
            (((0,), (0,)), ((), ())),
            preferred_element_type=jnp.float32,
        )
        for index in range(per_group):
            dense[pl.ds(group * per_group + index, height, stride=slots), :] = product[
                :, index * 128 : (index + 1) * 128
            ]

    per_batch = 128 // slots
    lane_group = lax.broadcasted_iota(jnp.int32, (8, 128), 1) // 32

    def batch(position, buffer):
        rows = dense[pl.ds(pl.multiple_of(position * 128, 128), 128), :]
        turned[buffer * 128 : (buffer + 1) * 128, :] = rows.T
        left = jnp.concatenate(
            [
                turned[pl.ds(buffer * 128 + 32 * part + quarter, 8, stride=4), :]
                for part in range(4)
                for quarter in range(4)
            ],
            axis=0,
        ).astype(jnp.bfloat16)
        gram = jnp.dot(
            left, spread(rows.astype(jnp.bfloat16), slots), preferred_element_type=jnp.float32
        )
        for index in range(per_batch):
            degree = position * per_batch + index
            factor = scale_ref[step * height + degree]
            for kind in range(2):
                result = None
                for turn in range(4):
                    first = 32 * (2 * kind) + 8 * ((2 * kind + turn) % 4)
                    second = 32 * (2 * kind + 1) + 8 * ((2 * kind + 1 + turn) % 4)
                    lanes = slice(index * 128, (index + 1) * 128)
                    value = jnp.where(
                        lane_group == 2 * kind,
                        gram[first : first + 8, lanes],
                        jnp.where(
                            lane_group == 2 * kind + 1, gram[second : second + 8, lanes], 0.0
                        ),
                    )
                    if turn > 0:
                        value = pltpu.roll(value, 32 * turn, axis=1)
                    result = value if result is None else result + value
                out_ref[pl.ds(degree * 16 + kind, 8, stride=2), :] = result * factor

    together = 4

    def several(position, carry):
        for buffer in range(together):
            batch(position * together + buffer, buffer)
        return carry

    lax.fori_loop(0, height // per_batch // together, several, 0)


def spectra_call(scale, gathered, stride, legendre_rows):
    row_count, degree_local = legendre_rows.shape
    columns = gathered.shape[1]
    inner = 2 * (gathered.shape[0] // stride)
    slots = row_count // inner
    height = 128
    result = pl.pallas_call(
        functools.partial(spectra_kernel, stride),
        grid=(degree_local // height,),
        in_specs=[
            pl.BlockSpec(memory_space=pltpu.SMEM),
            pl.BlockSpec(gathered.shape, lambda i: (0, 0)),
            pl.BlockSpec((row_count, height), lambda i: (0, i)),
        ],
        out_specs=pl.BlockSpec((height * 16, 128), lambda i: (i, 0)),
        out_shape=jax.ShapeDtypeStruct((degree_local * 16, 128), jnp.float32),
        scratch_shapes=[
            pltpu.VMEM(gathered.shape, jnp.float32),
            pltpu.VMEM((row_count, columns), jnp.bfloat16),
            pltpu.VMEM((height * slots, columns), jnp.float32),
            pltpu.VMEM((512, 128), jnp.float32),
        ],
        cost_estimate=pl.CostEstimate(
            flops=degree_local * slots * 4 * columns * columns,
            bytes_accessed=4 * degree_local * 2048,
            transcendentals=0,
        ),
    )(scale, gathered, legendre_rows)
    return (
        result.reshape(degree_local, 8, 2, 128)
        .transpose(0, 2, 1, 3)
        .reshape(degree_local, 2, 1024)
    )


def split_three(value):
    pieces = []
    rest = value
    for _ in range(3):
        piece = lax.reduce_precision(rest, 8, 7)
        pieces.append(piece)
        rest = rest - piece
    return pieces


def compact(sky_maps, sky_mask, pixel_counts, phi_offsets, low_orders, legendre):
    axes = ("band", "sub")
    devices = lax.axis_size(axes)
    device_index = lax.axis_index(axes)
    degree_count = legendre.shape[1]
    inner = legendre.shape[2]
    slots = 2 * low_orders.shape[0]
    orders = slot_orders(low_orders, degree_count)
    degree_local = degree_count // devices
    first_order = lax.dynamic_index_in_dim(low_orders, device_index, 0, keepdims=False)
    split_row = degree_count - first_order
    legendre_cols = legendre[0].T
    degrees = jnp.arange(degree_count, dtype=jnp.int32)[None, :]
    doubled = jnp.concatenate([legendre_cols, legendre_cols], axis=1)
    rolled = lax.dynamic_slice_in_dim(doubled, split_row, degree_count, 1)
    first = jnp.where(degrees >= first_order, rolled, 0.0).astype(jnp.bfloat16)
    second = jnp.where(degrees >= split_row, legendre_cols, 0.0).astype(jnp.bfloat16)
    sent = jnp.concatenate([first, second], axis=0)
    sent = sent.reshape(2 * inner, devices, degree_local).transpose(1, 0, 2)
    received = lax.all_to_all(sent, axes, split_axis=0, concat_axis=0, tiled=True)
    legendre_rows = received.reshape(slots * inner, degree_local)

    count = pixel_counts[0]
    valid = jnp.arange(sky_mask.shape[1], dtype=jnp.int32)[None, :] < count
    masked_weight = jnp.where(valid, sky_mask, 0.0)
    coefficients = fourier_call(sky_maps[0], masked_weight, count, phi_offsets[0], orders)
    square = split_three(jnp.sum(masked_weight * masked_weight))
    pixels = split_three(count.astype(jnp.float32))
    columns = coefficients.shape[1]
    extra = jnp.zeros((EXTRA, columns), jnp.float32)
    column_index = lax.broadcasted_iota(jnp.int32, (EXTRA, columns), 1)
    for index, piece in enumerate(square + pixels):
        extra = jnp.where(column_index == index, piece, extra)
    payload = jnp.concatenate([coefficients, extra.astype(jnp.bfloat16)], axis=0)
    gathered = lax.all_gather(payload, axes, axis=0, tiled=True)
    stride = slots + EXTRA
    pieces = gathered.reshape(devices, stride, columns)[:, slots, :6].astype(jnp.float32)
    weight = jnp.sum(pieces[:, :3]) / jnp.sum(pieces[:, 3:])
    scalars = jnp.stack([device_index.astype(jnp.int32), split_row])
    alm_packed = alm_call(scalars, gathered, stride, legendre_cols)
    own = device_index * degree_local + jnp.arange(degree_local, dtype=jnp.int32)
    counts = jnp.maximum(
        jnp.sum((orders[None, :] <= own[:, None]).astype(jnp.int32), axis=1), 1
    ).astype(jnp.float32)
    scale = 2.0 / (weight * counts)
    spectra = spectra_call(scale, gathered, stride, legendre_rows)
    return (alm_packed[None], spectra)


def general(sky_maps, sky_mask, pixel_counts, phi_offsets, low_orders, legendre):
    devices = lax.axis_size(("band", "sub"))
    device_index = lax.axis_index(("band", "sub"))
    degree_count = legendre.shape[1]
    orders = slot_orders(low_orders, degree_count)
    cycle_local = sky_maps.shape[0]
    maps_count = sky_maps.shape[2]
    pair_local = legendre.shape[0]
    slot_local = 2 * pair_local
    columns = 4 * maps_count
    valid_pixels = jnp.arange(sky_maps.shape[3], dtype=jnp.int32)[None, :] < pixel_counts[:, None]
    local_square = jnp.sum(jnp.where(valid_pixels, sky_mask * sky_mask, 0.0))
    local_pixels = jnp.sum(pixel_counts.astype(jnp.float32))
    total_square, total_pixels = lax.psum((local_square, local_pixels), ("band", "sub"))
    weight = total_square / total_pixels
    cycle_blocks = [
        cycle_fourier(sky_maps[0], sky_mask[0], pixel_counts[0], phi_offsets[0], orders)
    ]
    coefficients = jnp.stack(cycle_blocks, axis=1).reshape(
        devices, slot_local, cycle_local, columns
    )
    received = lax.all_to_all(
        coefficients, ("band", "sub"), split_axis=0, concat_axis=0, tiled=True
    )
    cycle_total = devices * cycle_local
    first_order = lax.dynamic_index_in_dim(
        low_orders, device_index * pair_local + 0, 0, keepdims=False
    )
    first_block = received[:, 0].reshape(cycle_total, columns)
    second_block = received[:, 1].reshape(cycle_total, columns)
    alm_pairs = [pair_alm(legendre[0], first_order, first_block, second_block)]
    alm_packed = jnp.stack(alm_pairs, axis=0)
    dense_local = dense_pair(alm_pairs[0], first_order)
    by_degree = lax.all_to_all(
        dense_local, ("band", "sub"), split_axis=1, concat_axis=0, tiled=True
    )
    degree_local = by_degree.shape[1]
    degrees = device_index * degree_local + jnp.arange(degree_local, dtype=jnp.int32)
    totals = outer_totals(by_degree, maps_count)
    spectra = scaled_spectra(totals, degrees, orders, weight, maps_count)
    return (alm_packed, spectra)


def local(sky_maps, sky_mask, pixel_counts, phi_offsets, low_orders, legendre):
    devices = lax.axis_size(("band", "sub"))
    fits = (
        sky_maps.shape[0] == 1
        and legendre.shape[0] == 1
        and sky_maps.shape[2] == 32
        and sky_maps.shape[3] % 2048 == 0
        and 2 * low_orders.shape[0] in (16, 32, 64)
        and legendre.shape[2] == 2 * devices
        and legendre.shape[2] in (16, 32, 64)
        and legendre.shape[1] % (128 * devices) == 0
        and legendre.shape[1] % 1024 == 0
    )
    body = compact if fits else general
    return body(sky_maps, sky_mask, pixel_counts, phi_offsets, low_orders, legendre)


def solution(mesh):
    placed = (
        P(("groups", "band", "sub"), None, None, None),
        P(("groups", "band", "sub"), None),
        P(("groups", "band", "sub")),
        P(("groups", "band", "sub")),
        P("groups"),
        P(("groups", "band", "sub"), None, None),
    )
    return jax.shard_map(
        local,
        mesh=mesh,
        in_specs=placed,
        out_specs=(
            P(("groups", "band", "sub"), None, None),
            P(("groups", "band", "sub"), None, None),
        ),
        check_vma=False,
    )
```

```python
import functools

import jax
import jax.numpy as jnp
from jax import lax
from jax.experimental import pallas as pl
from jax.experimental.pallas import tpu as pltpu
from jax.sharding import PartitionSpec as P


def slot_orders(low_orders, degree_count):
    return jnp.stack([low_orders, degree_count - low_orders], axis=1).reshape(-1)


def finish_cycle(pixel_sums, cycle_count, orders):
    slots = orders.shape[0]
    maps_count = pixel_sums.shape[1] // 2
    inverse_root = 1.0 / jnp.sqrt(cycle_count.astype(jnp.float32))
    real_part = (pixel_sums[:slots] * inverse_root).reshape(slots, 2, maps_count)
    imag_part = (-pixel_sums[slots:] * inverse_root).reshape(slots, 2, maps_count)
    joined = jnp.stack(
        [real_part[:, 0], imag_part[:, 0], real_part[:, 1], imag_part[:, 1]], axis=1
    ).reshape(slots, 4 * maps_count)
    live_slots = 2 * orders < cycle_count
    return jnp.where(live_slots[:, None], joined, 0.0).astype(jnp.bfloat16)


def cycle_fourier(cycle_maps, cycle_mask, cycle_count, cycle_offset, orders):
    maps_count = cycle_maps.shape[1]
    pixel_slots = cycle_maps.shape[2]
    cycle_rows = cycle_maps.reshape(2 * maps_count, pixel_slots)
    block_width = min(2048, pixel_slots)
    group_count = block_width // 128
    slots = orders.shape[0]
    modulus = 2 * cycle_count
    scale = jnp.pi / cycle_count.astype(jnp.float32)
    order_mod = orders % modulus
    fine_units = 2 * order_mod[:, None] * jnp.arange(128, dtype=jnp.int32)[None, :] % modulus
    fine_angle = scale * fine_units.astype(jnp.float32)
    fine_cos = jnp.cos(fine_angle)[:, None, :]
    fine_sin = jnp.sin(fine_angle)[:, None, :]

    def add_block(block_index, totals):
        first_pixel = block_index * block_width
        row_block = lax.dynamic_slice_in_dim(cycle_rows, first_pixel, block_width, 1)
        mask_block = lax.dynamic_slice_in_dim(cycle_mask, first_pixel, block_width, 0)
        pixels = first_pixel + jnp.arange(block_width, dtype=jnp.int32)
        masked = jnp.where(
            pixels[None, :] < cycle_count, mask_block[None, :] * row_block.astype(jnp.float32), 0.0
        ).astype(jnp.bfloat16)
        group_starts = first_pixel + 128 * jnp.arange(group_count, dtype=jnp.int32)
        coarse_units = (
            order_mod[:, None] * ((2 * group_starts[None, :] + cycle_offset) % modulus) % modulus
        )
        coarse_angle = scale * coarse_units.astype(jnp.float32)
        coarse_cos = jnp.cos(coarse_angle)[:, :, None]
        coarse_sin = jnp.sin(coarse_angle)[:, :, None]
        cosines = (coarse_cos * fine_cos - coarse_sin * fine_sin).reshape(slots, block_width)
        sines = (coarse_sin * fine_cos + coarse_cos * fine_sin).reshape(slots, block_width)
        tables = jnp.concatenate([cosines.astype(jnp.bfloat16), sines.astype(jnp.bfloat16)], axis=0)
        return totals + lax.dot_general(
            tables, masked, (((1,), (1,)), ((), ())), preferred_element_type=jnp.float32
        )

    block_count = (cycle_count + block_width - 1) // block_width
    pixel_sums = lax.fori_loop(
        0, block_count, add_block, jnp.zeros((2 * slots, 2 * maps_count), jnp.float32)
    )
    return finish_cycle(pixel_sums, cycle_count, orders)


def stacked_operand(block_rows):
    quarter = block_rows.shape[1] // 4
    q_real = block_rows[:, :quarter]
    q_imag = block_rows[:, quarter : 2 * quarter]
    u_real = block_rows[:, 2 * quarter : 3 * quarter]
    u_imag = block_rows[:, 3 * quarter :]
    lower_half = jnp.concatenate([u_imag, -u_real, -q_imag, q_real], axis=1)
    return jnp.concatenate([block_rows, lower_half], axis=0)


def pair_alm(legendre_rows, first_order, first_block, second_block):
    first_operand = stacked_operand(first_block)
    second_operand = stacked_operand(second_block)
    degree_count, inner_width = legendre_rows.shape
    tile_height = min(128, degree_count)
    tile_count = degree_count // tile_height
    split_row = degree_count - first_order
    tile_starts = jnp.arange(tile_count, dtype=jnp.int32) * tile_height
    chosen = jnp.where(
        (tile_starts < split_row)[:, None, None], first_operand[None], second_operand[None]
    )
    tile_product = jnp.einsum(
        "tir,tro->tio",
        legendre_rows.reshape(tile_count, tile_height, inner_width),
        chosen,
        preferred_element_type=jnp.float32,
    )
    tile_product = tile_product.reshape(degree_count, first_operand.shape[1])
    border = split_row // tile_height * tile_height
    border_rows = lax.dynamic_slice_in_dim(legendre_rows, border, tile_height, 0)
    border_product = jnp.dot(border_rows, second_operand, preferred_element_type=jnp.float32)
    current = lax.dynamic_slice_in_dim(tile_product, border, tile_height, 0)
    row_index = border + jnp.arange(tile_height, dtype=jnp.int32)
    patched = jnp.where((row_index >= split_row)[:, None], border_product, current)
    return -lax.dynamic_update_slice_in_dim(tile_product, patched, border, 0)


def dense_pair(alm_rows, first_order):
    degree_count = alm_rows.shape[0]
    degrees = jnp.arange(degree_count, dtype=jnp.int32)
    first_dense = jnp.where(
        (degrees >= first_order)[:, None], jnp.roll(alm_rows, first_order, axis=0), 0.0
    ).astype(jnp.bfloat16)
    second_dense = jnp.where(
        (degrees >= degree_count - first_order)[:, None], alm_rows, 0.0
    ).astype(jnp.bfloat16)
    return jnp.stack([first_dense, second_dense], axis=0)


def outer_totals(rows, maps_count):
    split_parts = rows.reshape(rows.shape[0], rows.shape[1], 2, 2, maps_count)
    return jnp.einsum(
        "slerm,slern->lemn", split_parts, split_parts, preferred_element_type=jnp.float32
    )


def scaled_spectra(totals, degrees, orders, weight, maps_count):
    counts = jnp.maximum(
        jnp.sum((orders[None, :] <= degrees[:, None]).astype(jnp.int32), axis=1), 1
    ).astype(jnp.float32)
    return (2.0 * totals / (weight * counts)[:, None, None, None]).reshape(
        degrees.shape[0], 2, maps_count * maps_count
    )


EXTRA = 16


def fourier_kernel(maps_ref, mask_ref, fine_ref, coarse_ref, live_ref, out_ref, total):
    step = pl.program_id(0)
    slots = fine_ref.shape[1]
    groups = maps_ref.shape[1] // 128
    fine_cos = fine_ref[0]
    fine_sin = fine_ref[1]
    cosines = []
    sines = []
    for group in range(groups):
        coarse_cos = coarse_ref[0, 0, :, group : group + 1]
        coarse_sin = coarse_ref[1, 0, :, group : group + 1]
        cosines.append((coarse_cos * fine_cos - coarse_sin * fine_sin).astype(jnp.bfloat16))
        sines.append((coarse_sin * fine_cos + coarse_cos * fine_sin).astype(jnp.bfloat16))
    tables = jnp.concatenate(
        [jnp.concatenate(cosines, axis=1), jnp.concatenate(sines, axis=1)], axis=0
    )
    masked = (maps_ref[...].astype(jnp.float32) * mask_ref[...]).astype(jnp.bfloat16)
    sums = lax.dot_general(
        tables, masked, (((1,), (1,)), ((), ())), preferred_element_type=jnp.float32
    )

    @pl.when(step == 0)
    def _():
        total[...] = sums

    @pl.when(step > 0)
    def _():
        total[...] += sums

    @pl.when(step == pl.num_programs(0) - 1)
    def _():
        half = maps_ref.shape[0] // 2
        real = total[:slots]
        imag = -total[slots:]
        joined = jnp.concatenate(
            [real[:, :half], imag[:, :half], real[:, half:], imag[:, half:]], axis=1
        )
        out_ref[...] = (joined * live_ref[...]).astype(jnp.bfloat16)


def fourier_call(cycle_maps, masked_weight, cycle_count, cycle_offset, orders):
    maps_count = cycle_maps.shape[1]
    pixel_slots = cycle_maps.shape[2]
    rows = cycle_maps.reshape(2 * maps_count, pixel_slots)
    slots = orders.shape[0]
    width = min(2048, pixel_slots)
    blocks = pixel_slots // width
    groups = width // 128
    modulus = 2 * cycle_count
    scale = jnp.pi / cycle_count.astype(jnp.float32)
    order_mod = orders % modulus
    fine_units = 2 * order_mod[:, None] * jnp.arange(128, dtype=jnp.int32)[None, :] % modulus
    starts = 128 * jnp.arange(blocks * groups, dtype=jnp.int32)
    starts = ((2 * starts + cycle_offset) % modulus).reshape(blocks, 1, groups)
    coarse_units = order_mod[None, :, None] * starts % modulus
    fine_angle = scale * fine_units.astype(jnp.float32)
    coarse_angle = scale * coarse_units.astype(jnp.float32)
    fine = jnp.stack([jnp.cos(fine_angle), jnp.sin(fine_angle)])
    coarse = jnp.stack([jnp.cos(coarse_angle), jnp.sin(coarse_angle)])
    inverse_root = 1.0 / jnp.sqrt(cycle_count.astype(jnp.float32))
    live = jnp.broadcast_to(
        jnp.where(2 * orders < cycle_count, inverse_root, 0.0)[:, None], (slots, 4 * maps_count)
    )
    return pl.pallas_call(
        fourier_kernel,
        grid=(blocks,),
        in_specs=[
            pl.BlockSpec((2 * maps_count, width), lambda i: (0, i)),
            pl.BlockSpec((1, width), lambda i: (0, i)),
            pl.BlockSpec((2, slots, 128), lambda i: (0, 0, 0)),
            pl.BlockSpec((2, 1, slots, groups), lambda i: (0, i, 0, 0)),
            pl.BlockSpec((slots, 4 * maps_count), lambda i: (0, 0)),
        ],
        out_specs=pl.BlockSpec((slots, 4 * maps_count), lambda i: (0, 0)),
        out_shape=jax.ShapeDtypeStruct((slots, 4 * maps_count), jnp.bfloat16),
        scratch_shapes=[pltpu.VMEM((2 * slots, 2 * maps_count), jnp.float32)],
        cost_estimate=pl.CostEstimate(
            flops=8 * slots * maps_count * pixel_slots,
            bytes_accessed=4 * maps_count * pixel_slots,
            transcendentals=0,
        ),
    )(rows, masked_weight, fine, coarse, live)


def operand_rows(wide, slot, cycles, stride):
    upper = wide[pl.ds(slot, cycles, stride=stride), :]
    quarter = upper.shape[1] // 4
    lower = jnp.concatenate(
        [
            upper[:, 3 * quarter :],
            -upper[:, 2 * quarter : 3 * quarter],
            -upper[:, quarter : 2 * quarter],
            upper[:, :quarter],
        ],
        axis=1,
    )
    return jnp.concatenate([upper, lower], axis=0)


def alm_kernel(stride, scalar_ref, gathered_ref, legendre_ref, out_ref, wide, operand):
    step = pl.program_id(0)
    height = out_ref.shape[0]
    columns = out_ref.shape[1]
    cycles = gathered_ref.shape[0] // stride

    @pl.when(step == 0)
    def _():
        wide[...] = gathered_ref[...].astype(jnp.float32)
        pair = scalar_ref[0]
        operand[...] = -jnp.concatenate(
            [
                operand_rows(wide, 2 * pair, cycles, stride),
                operand_rows(wide, 2 * pair + 1, cycles, stride),
            ],
            axis=1,
        )

    product = lax.dot_general(
        legendre_ref[...],
        operand[...].astype(jnp.bfloat16),
        (((0,), (0,)), ((), ())),
        preferred_element_type=jnp.float32,
    )
    row = step * height + lax.broadcasted_iota(jnp.int32, (height, columns), 0)
    out_ref[...] = jnp.where(row < scalar_ref[1], product[:, :columns], product[:, columns:])


def alm_call(scalars, gathered, stride, legendre_cols):
    inner, degree_count = legendre_cols.shape
    columns = gathered.shape[1]
    height = min(1024, degree_count)
    return pl.pallas_call(
        functools.partial(alm_kernel, stride),
        grid=(degree_count // height,),
        in_specs=[
            pl.BlockSpec(memory_space=pltpu.SMEM),
            pl.BlockSpec(gathered.shape, lambda i: (0, 0)),
            pl.BlockSpec((inner, height), lambda i: (0, i)),
        ],
        out_specs=pl.BlockSpec((height, columns), lambda i: (i, 0)),
        out_shape=jax.ShapeDtypeStruct((degree_count, columns), jnp.float32),
        scratch_shapes=[
            pltpu.VMEM(gathered.shape, jnp.float32),
            pltpu.VMEM((inner, 2 * columns), jnp.float32),
        ],
        cost_estimate=pl.CostEstimate(
            flops=4 * degree_count * inner * columns,
            bytes_accessed=4 * degree_count * columns,
            transcendentals=0,
        ),
    )(scalars, gathered, legendre_cols)


def spectra_kernel(stride, scale_ref, gathered_ref, legendre_ref, out_ref, wide, operands, dense, turned):
    step = pl.program_id(0)
    cycles = gathered_ref.shape[0] // stride
    inner = 2 * cycles
    slots = legendre_ref.shape[0] // inner
    height = legendre_ref.shape[1]
    per_group = 128 // inner
    group_count = slots // per_group

    @pl.when(step == 0)
    def _():
        wide[...] = gathered_ref[...].astype(jnp.float32)
        for slot in range(slots):
            operands[slot * inner : (slot + 1) * inner, :] = operand_rows(
                wide, slot, cycles, stride
            ).astype(jnp.bfloat16)

    def spread(tall, piece):
        parts = []
        for index in range(128 // piece):
            own = tall[index * piece : (index + 1) * piece]
            column = []
            if index > 0:
                column.append(jnp.zeros((index * piece, 128), tall.dtype))
            column.append(own)
            if (index + 1) * piece < 128:
                column.append(jnp.zeros((128 - (index + 1) * piece, 128), tall.dtype))
            parts.append(jnp.concatenate(column, axis=0))
        return jnp.concatenate(parts, axis=1)

    for group in range(group_count):
        wide_operand = spread(operands[group * 128 : (group + 1) * 128, :], inner)
        product = lax.dot_general(
            legendre_ref[group * 128 : (group + 1) * 128, :],
            wide_operand,
            (((0,), (0,)), ((), ())),
            preferred_element_type=jnp.float32,
        )
        for index in range(per_group):
            dense[pl.ds(group * per_group + index, height, stride=slots), :] = product[
                :, index * 128 : (index + 1) * 128
            ]

    per_batch = 128 // slots
    lane_group = lax.broadcasted_iota(jnp.int32, (8, 128), 1) // 32

    def batch(position, buffer):
        rows = dense[pl.ds(pl.multiple_of(position * 128, 128), 128), :]
        turned[buffer * 128 : (buffer + 1) * 128, :] = rows.T
        left = jnp.concatenate(
            [
                turned[pl.ds(buffer * 128 + 32 * part + quarter, 8, stride=4), :]
                for part in range(4)
                for quarter in range(4)
            ],
            axis=0,
        ).astype(jnp.bfloat16)
        gram = jnp.dot(
            left, spread(rows.astype(jnp.bfloat16), slots), preferred_element_type=jnp.float32
        )
        for index in range(per_batch):
            degree = position * per_batch + index
            factor = scale_ref[step * height + degree]
            for kind in range(2):
                result = None
                for turn in range(4):
                    first = 32 * (2 * kind) + 8 * ((2 * kind + turn) % 4)
                    second = 32 * (2 * kind + 1) + 8 * ((2 * kind + 1 + turn) % 4)
                    lanes = slice(index * 128, (index + 1) * 128)
                    value = jnp.where(
                        lane_group == 2 * kind,
                        gram[first : first + 8, lanes],
                        jnp.where(
                            lane_group == 2 * kind + 1, gram[second : second + 8, lanes], 0.0
                        ),
                    )
                    if turn > 0:
                        value = pltpu.roll(value, 32 * turn, axis=1)
                    result = value if result is None else result + value
                out_ref[pl.ds(degree * 16 + kind, 8, stride=2), :] = result * factor

    together = 4

    def several(position, carry):
        for buffer in range(together):
            batch(position * together + buffer, buffer)
        return carry

    lax.fori_loop(0, height // per_batch // together, several, 0)


def spectra_call(scale, gathered, stride, legendre_rows):
    row_count, degree_local = legendre_rows.shape
    columns = gathered.shape[1]
    inner = 2 * (gathered.shape[0] // stride)
    slots = row_count // inner
    height = 128
    result = pl.pallas_call(
        functools.partial(spectra_kernel, stride),
        grid=(degree_local // height,),
        in_specs=[
            pl.BlockSpec(memory_space=pltpu.SMEM),
            pl.BlockSpec(gathered.shape, lambda i: (0, 0)),
            pl.BlockSpec((row_count, height), lambda i: (0, i)),
        ],
        out_specs=pl.BlockSpec((height * 16, 128), lambda i: (i, 0)),
        out_shape=jax.ShapeDtypeStruct((degree_local * 16, 128), jnp.float32),
        scratch_shapes=[
            pltpu.VMEM(gathered.shape, jnp.float32),
            pltpu.VMEM((row_count, columns), jnp.bfloat16),
            pltpu.VMEM((height * slots, columns), jnp.float32),
            pltpu.VMEM((512, 128), jnp.float32),
        ],
        cost_estimate=pl.CostEstimate(
            flops=degree_local * slots * 4 * columns * columns,
            bytes_accessed=4 * degree_local * 2048,
            transcendentals=0,
        ),
    )(scale, gathered, legendre_rows)
    return (
        result.reshape(degree_local, 8, 2, 128)
        .transpose(0, 2, 1, 3)
        .reshape(degree_local, 2, 1024)
    )


def gather_kernel(devices, subs, payload_ref, out_ref, send_sem, recv_sem):
    me = lax.axis_index("band") * subs + lax.axis_index("sub")
    rows = payload_ref.shape[0]

    def place(index):
        return {"band": index // subs, "sub": index % subs}

    def slot(index):
        return out_ref.at[pl.ds(pl.multiple_of(index * rows, rows), rows), :]

    barrier = pltpu.get_barrier_semaphore()
    for offset in range(1, devices):
        pl.semaphore_signal(
            barrier,
            inc=1,
            device_id=place((me + offset) % devices),
            device_id_type=pl.DeviceIdType.MESH,
        )
    pl.semaphore_wait(barrier, devices - 1)

    def copy_of(offset, source):
        return pltpu.make_async_remote_copy(
            src_ref=payload_ref,
            dst_ref=slot(source),
            send_sem=send_sem.at[offset],
            recv_sem=recv_sem.at[offset],
            device_id=place((me + offset) % devices),
            device_id_type=pl.DeviceIdType.MESH,
        )

    for offset in range(1, devices):
        copy_of(offset, me).start()
    out_ref[pl.ds(pl.multiple_of(me * rows, rows), rows), :] = payload_ref[...]
    for offset in range(1, devices):
        copy_of(offset, (me + devices - offset) % devices).wait_recv()
    for offset in range(1, devices):
        copy_of(offset, me).wait_send()


def gather_call(payload, devices, subs):
    rows, columns = payload.shape
    return pl.pallas_call(
        functools.partial(gather_kernel, devices, subs),
        in_specs=[pl.BlockSpec(memory_space=pltpu.VMEM)],
        out_specs=pl.BlockSpec(memory_space=pltpu.VMEM),
        out_shape=jax.ShapeDtypeStruct((devices * rows, columns), payload.dtype),
        scratch_shapes=[
            pltpu.SemaphoreType.DMA((devices,)),
            pltpu.SemaphoreType.DMA((devices,)),
        ],
        compiler_params=pltpu.CompilerParams(collective_id=0, has_side_effects=True),
    )(payload)


def split_three(value):
    pieces = []
    rest = value
    for _ in range(3):
        piece = lax.reduce_precision(rest, 8, 7)
        pieces.append(piece)
        rest = rest - piece
    return pieces


def compact(sky_maps, sky_mask, pixel_counts, phi_offsets, low_orders, legendre):
    axes = ("band", "sub")
    devices = lax.axis_size(axes)
    device_index = lax.axis_index(axes)
    degree_count = legendre.shape[1]
    inner = legendre.shape[2]
    slots = 2 * low_orders.shape[0]
    orders = slot_orders(low_orders, degree_count)
    degree_local = degree_count // devices
    first_order = lax.dynamic_index_in_dim(low_orders, device_index, 0, keepdims=False)
    split_row = degree_count - first_order
    legendre_cols = legendre[0].T
    degrees = jnp.arange(degree_count, dtype=jnp.int32)[None, :]
    doubled = jnp.concatenate([legendre_cols, legendre_cols], axis=1)
    rolled = lax.dynamic_slice_in_dim(doubled, split_row, degree_count, 1)
    first = jnp.where(degrees >= first_order, rolled, 0.0).astype(jnp.bfloat16)
    second = jnp.where(degrees >= split_row, legendre_cols, 0.0).astype(jnp.bfloat16)
    sent = jnp.concatenate([first, second], axis=0)
    sent = sent.reshape(2 * inner, devices, degree_local).transpose(1, 0, 2)
    received = lax.all_to_all(sent, axes, split_axis=0, concat_axis=0, tiled=True)
    legendre_rows = received.reshape(slots * inner, degree_local)

    count = pixel_counts[0]
    valid = jnp.arange(sky_mask.shape[1], dtype=jnp.int32)[None, :] < count
    masked_weight = jnp.where(valid, sky_mask, 0.0)
    coefficients = fourier_call(sky_maps[0], masked_weight, count, phi_offsets[0], orders)
    square = split_three(jnp.sum(masked_weight * masked_weight))
    pixels = split_three(count.astype(jnp.float32))
    columns = coefficients.shape[1]
    extra = jnp.zeros((EXTRA, columns), jnp.float32)
    column_index = lax.broadcasted_iota(jnp.int32, (EXTRA, columns), 1)
    for index, piece in enumerate(square + pixels):
        extra = jnp.where(column_index == index, piece, extra)
    payload = jnp.concatenate([coefficients, extra.astype(jnp.bfloat16)], axis=0)
    gathered = gather_call(payload, devices, lax.axis_size("sub"))
    stride = slots + EXTRA
    pieces = gathered.reshape(devices, stride, columns)[:, slots, :6].astype(jnp.float32)
    weight = jnp.sum(pieces[:, :3]) / jnp.sum(pieces[:, 3:])
    scalars = jnp.stack([device_index.astype(jnp.int32), split_row])
    alm_packed = alm_call(scalars, gathered, stride, legendre_cols)
    own = device_index * degree_local + jnp.arange(degree_local, dtype=jnp.int32)
    counts = jnp.maximum(
        jnp.sum((orders[None, :] <= own[:, None]).astype(jnp.int32), axis=1), 1
    ).astype(jnp.float32)
    scale = 2.0 / (weight * counts)
    spectra = spectra_call(scale, gathered, stride, legendre_rows)
    return (alm_packed[None], spectra)


def general(sky_maps, sky_mask, pixel_counts, phi_offsets, low_orders, legendre):
    devices = lax.axis_size(("band", "sub"))
    device_index = lax.axis_index(("band", "sub"))
    degree_count = legendre.shape[1]
    orders = slot_orders(low_orders, degree_count)
    cycle_local = sky_maps.shape[0]
    maps_count = sky_maps.shape[2]
    pair_local = legendre.shape[0]
    slot_local = 2 * pair_local
    columns = 4 * maps_count
    valid_pixels = jnp.arange(sky_maps.shape[3], dtype=jnp.int32)[None, :] < pixel_counts[:, None]
    local_square = jnp.sum(jnp.where(valid_pixels, sky_mask * sky_mask, 0.0))
    local_pixels = jnp.sum(pixel_counts.astype(jnp.float32))
    total_square, total_pixels = lax.psum((local_square, local_pixels), ("band", "sub"))
    weight = total_square / total_pixels
    cycle_blocks = [
        cycle_fourier(sky_maps[0], sky_mask[0], pixel_counts[0], phi_offsets[0], orders)
    ]
    coefficients = jnp.stack(cycle_blocks, axis=1).reshape(
        devices, slot_local, cycle_local, columns
    )
    received = lax.all_to_all(
        coefficients, ("band", "sub"), split_axis=0, concat_axis=0, tiled=True
    )
    cycle_total = devices * cycle_local
    first_order = lax.dynamic_index_in_dim(
        low_orders, device_index * pair_local + 0, 0, keepdims=False
    )
    first_block = received[:, 0].reshape(cycle_total, columns)
    second_block = received[:, 1].reshape(cycle_total, columns)
    alm_pairs = [pair_alm(legendre[0], first_order, first_block, second_block)]
    alm_packed = jnp.stack(alm_pairs, axis=0)
    dense_local = dense_pair(alm_pairs[0], first_order)
    by_degree = lax.all_to_all(
        dense_local, ("band", "sub"), split_axis=1, concat_axis=0, tiled=True
    )
    degree_local = by_degree.shape[1]
    degrees = device_index * degree_local + jnp.arange(degree_local, dtype=jnp.int32)
    totals = outer_totals(by_degree, maps_count)
    spectra = scaled_spectra(totals, degrees, orders, weight, maps_count)
    return (alm_packed, spectra)


def local(sky_maps, sky_mask, pixel_counts, phi_offsets, low_orders, legendre):
    devices = lax.axis_size(("band", "sub"))
    fits = (
        sky_maps.shape[0] == 1
        and legendre.shape[0] == 1
        and sky_maps.shape[2] == 32
        and sky_maps.shape[3] % 2048 == 0
        and 2 * low_orders.shape[0] in (16, 32, 64)
        and legendre.shape[2] == 2 * devices
        and legendre.shape[2] in (16, 32, 64)
        and legendre.shape[1] % (128 * devices) == 0
        and legendre.shape[1] % 1024 == 0
    )
    body = compact if fits else general
    return body(sky_maps, sky_mask, pixel_counts, phi_offsets, low_orders, legendre)


def solution(mesh):
    placed = (
        P(("groups", "band", "sub"), None, None, None),
        P(("groups", "band", "sub"), None),
        P(("groups", "band", "sub")),
        P(("groups", "band", "sub")),
        P("groups"),
        P(("groups", "band", "sub"), None, None),
    )
    return jax.shard_map(
        local,
        mesh=mesh,
        in_specs=placed,
        out_specs=(
            P(("groups", "band", "sub"), None, None),
            P(("groups", "band", "sub"), None, None),
        ),
        check_vma=False,
    )
```

```python
import functools

import jax
import jax.numpy as jnp
from jax import lax
from jax.experimental import pallas as pl
from jax.experimental.pallas import tpu as pltpu
from jax.sharding import PartitionSpec as P


def slot_orders(low_orders, degree_count):
    return jnp.stack([low_orders, degree_count - low_orders], axis=1).reshape(-1)


def finish_cycle(pixel_sums, cycle_count, orders):
    slots = orders.shape[0]
    maps_count = pixel_sums.shape[1] // 2
    inverse_root = 1.0 / jnp.sqrt(cycle_count.astype(jnp.float32))
    real_part = (pixel_sums[:slots] * inverse_root).reshape(slots, 2, maps_count)
    imag_part = (-pixel_sums[slots:] * inverse_root).reshape(slots, 2, maps_count)
    joined = jnp.stack(
        [real_part[:, 0], imag_part[:, 0], real_part[:, 1], imag_part[:, 1]], axis=1
    ).reshape(slots, 4 * maps_count)
    live_slots = 2 * orders < cycle_count
    return jnp.where(live_slots[:, None], joined, 0.0).astype(jnp.bfloat16)


def cycle_fourier(cycle_maps, cycle_mask, cycle_count, cycle_offset, orders):
    maps_count = cycle_maps.shape[1]
    pixel_slots = cycle_maps.shape[2]
    cycle_rows = cycle_maps.reshape(2 * maps_count, pixel_slots)
    block_width = min(2048, pixel_slots)
    group_count = block_width // 128
    slots = orders.shape[0]
    modulus = 2 * cycle_count
    scale = jnp.pi / cycle_count.astype(jnp.float32)
    order_mod = orders % modulus
    fine_units = 2 * order_mod[:, None] * jnp.arange(128, dtype=jnp.int32)[None, :] % modulus
    fine_angle = scale * fine_units.astype(jnp.float32)
    fine_cos = jnp.cos(fine_angle)[:, None, :]
    fine_sin = jnp.sin(fine_angle)[:, None, :]

    def add_block(block_index, totals):
        first_pixel = block_index * block_width
        row_block = lax.dynamic_slice_in_dim(cycle_rows, first_pixel, block_width, 1)
        mask_block = lax.dynamic_slice_in_dim(cycle_mask, first_pixel, block_width, 0)
        pixels = first_pixel + jnp.arange(block_width, dtype=jnp.int32)
        masked = jnp.where(
            pixels[None, :] < cycle_count, mask_block[None, :] * row_block.astype(jnp.float32), 0.0
        ).astype(jnp.bfloat16)
        group_starts = first_pixel + 128 * jnp.arange(group_count, dtype=jnp.int32)
        coarse_units = (
            order_mod[:, None] * ((2 * group_starts[None, :] + cycle_offset) % modulus) % modulus
        )
        coarse_angle = scale * coarse_units.astype(jnp.float32)
        coarse_cos = jnp.cos(coarse_angle)[:, :, None]
        coarse_sin = jnp.sin(coarse_angle)[:, :, None]
        cosines = (coarse_cos * fine_cos - coarse_sin * fine_sin).reshape(slots, block_width)
        sines = (coarse_sin * fine_cos + coarse_cos * fine_sin).reshape(slots, block_width)
        tables = jnp.concatenate([cosines.astype(jnp.bfloat16), sines.astype(jnp.bfloat16)], axis=0)
        return totals + lax.dot_general(
            tables, masked, (((1,), (1,)), ((), ())), preferred_element_type=jnp.float32
        )

    block_count = (cycle_count + block_width - 1) // block_width
    pixel_sums = lax.fori_loop(
        0, block_count, add_block, jnp.zeros((2 * slots, 2 * maps_count), jnp.float32)
    )
    return finish_cycle(pixel_sums, cycle_count, orders)


def stacked_operand(block_rows):
    quarter = block_rows.shape[1] // 4
    q_real = block_rows[:, :quarter]
    q_imag = block_rows[:, quarter : 2 * quarter]
    u_real = block_rows[:, 2 * quarter : 3 * quarter]
    u_imag = block_rows[:, 3 * quarter :]
    lower_half = jnp.concatenate([u_imag, -u_real, -q_imag, q_real], axis=1)
    return jnp.concatenate([block_rows, lower_half], axis=0)


def pair_alm(legendre_rows, first_order, first_block, second_block):
    first_operand = stacked_operand(first_block)
    second_operand = stacked_operand(second_block)
    degree_count, inner_width = legendre_rows.shape
    tile_height = min(128, degree_count)
    tile_count = degree_count // tile_height
    split_row = degree_count - first_order
    tile_starts = jnp.arange(tile_count, dtype=jnp.int32) * tile_height
    chosen = jnp.where(
        (tile_starts < split_row)[:, None, None], first_operand[None], second_operand[None]
    )
    tile_product = jnp.einsum(
        "tir,tro->tio",
        legendre_rows.reshape(tile_count, tile_height, inner_width),
        chosen,
        preferred_element_type=jnp.float32,
    )
    tile_product = tile_product.reshape(degree_count, first_operand.shape[1])
    border = split_row // tile_height * tile_height
    border_rows = lax.dynamic_slice_in_dim(legendre_rows, border, tile_height, 0)
    border_product = jnp.dot(border_rows, second_operand, preferred_element_type=jnp.float32)
    current = lax.dynamic_slice_in_dim(tile_product, border, tile_height, 0)
    row_index = border + jnp.arange(tile_height, dtype=jnp.int32)
    patched = jnp.where((row_index >= split_row)[:, None], border_product, current)
    return -lax.dynamic_update_slice_in_dim(tile_product, patched, border, 0)


def dense_pair(alm_rows, first_order):
    degree_count = alm_rows.shape[0]
    degrees = jnp.arange(degree_count, dtype=jnp.int32)
    first_dense = jnp.where(
        (degrees >= first_order)[:, None], jnp.roll(alm_rows, first_order, axis=0), 0.0
    ).astype(jnp.bfloat16)
    second_dense = jnp.where(
        (degrees >= degree_count - first_order)[:, None], alm_rows, 0.0
    ).astype(jnp.bfloat16)
    return jnp.stack([first_dense, second_dense], axis=0)


def outer_totals(rows, maps_count):
    split_parts = rows.reshape(rows.shape[0], rows.shape[1], 2, 2, maps_count)
    return jnp.einsum(
        "slerm,slern->lemn", split_parts, split_parts, preferred_element_type=jnp.float32
    )


def scaled_spectra(totals, degrees, orders, weight, maps_count):
    counts = jnp.maximum(
        jnp.sum((orders[None, :] <= degrees[:, None]).astype(jnp.int32), axis=1), 1
    ).astype(jnp.float32)
    return (2.0 * totals / (weight * counts)[:, None, None, None]).reshape(
        degrees.shape[0], 2, maps_count * maps_count
    )


EXTRA = 16


def fourier_kernel(maps_ref, mask_ref, fine_ref, coarse_ref, live_ref, out_ref, total):
    step = pl.program_id(0)
    slots = fine_ref.shape[1]
    groups = maps_ref.shape[1] // 128
    fine_cos = fine_ref[0]
    fine_sin = fine_ref[1]
    cosines = []
    sines = []
    for group in range(groups):
        coarse_cos = coarse_ref[0, 0, :, group : group + 1]
        coarse_sin = coarse_ref[1, 0, :, group : group + 1]
        cosines.append((coarse_cos * fine_cos - coarse_sin * fine_sin).astype(jnp.bfloat16))
        sines.append((coarse_sin * fine_cos + coarse_cos * fine_sin).astype(jnp.bfloat16))
    tables = jnp.concatenate(
        [jnp.concatenate(cosines, axis=1), jnp.concatenate(sines, axis=1)], axis=0
    )
    masked = (maps_ref[...].astype(jnp.float32) * mask_ref[...]).astype(jnp.bfloat16)
    sums = lax.dot_general(
        tables, masked, (((1,), (1,)), ((), ())), preferred_element_type=jnp.float32
    )

    @pl.when(step == 0)
    def _():
        total[...] = sums

    @pl.when(step > 0)
    def _():
        total[...] += sums

    @pl.when(step == pl.num_programs(0) - 1)
    def _():
        half = maps_ref.shape[0] // 2
        real = total[:slots]
        imag = -total[slots:]
        joined = jnp.concatenate(
            [real[:, :half], imag[:, :half], real[:, half:], imag[:, half:]], axis=1
        )
        out_ref[...] = (joined * live_ref[...]).astype(jnp.bfloat16)


def fourier_call(cycle_maps, masked_weight, cycle_count, cycle_offset, orders):
    maps_count = cycle_maps.shape[1]
    pixel_slots = cycle_maps.shape[2]
    rows = cycle_maps.reshape(2 * maps_count, pixel_slots)
    slots = orders.shape[0]
    width = min(2048, pixel_slots)
    blocks = pixel_slots // width
    groups = width // 128
    modulus = 2 * cycle_count
    scale = jnp.pi / cycle_count.astype(jnp.float32)
    order_mod = orders % modulus
    fine_units = 2 * order_mod[:, None] * jnp.arange(128, dtype=jnp.int32)[None, :] % modulus
    starts = 128 * jnp.arange(blocks * groups, dtype=jnp.int32)
    starts = ((2 * starts + cycle_offset) % modulus).reshape(blocks, 1, groups)
    coarse_units = order_mod[None, :, None] * starts % modulus
    fine_angle = scale * fine_units.astype(jnp.float32)
    coarse_angle = scale * coarse_units.astype(jnp.float32)
    fine = jnp.stack([jnp.cos(fine_angle), jnp.sin(fine_angle)])
    coarse = jnp.stack([jnp.cos(coarse_angle), jnp.sin(coarse_angle)])
    inverse_root = 1.0 / jnp.sqrt(cycle_count.astype(jnp.float32))
    live = jnp.broadcast_to(
        jnp.where(2 * orders < cycle_count, inverse_root, 0.0)[:, None], (slots, 4 * maps_count)
    )
    return pl.pallas_call(
        fourier_kernel,
        grid=(blocks,),
        in_specs=[
            pl.BlockSpec((2 * maps_count, width), lambda i: (0, i)),
            pl.BlockSpec((1, width), lambda i: (0, i)),
            pl.BlockSpec((2, slots, 128), lambda i: (0, 0, 0)),
            pl.BlockSpec((2, 1, slots, groups), lambda i: (0, i, 0, 0)),
            pl.BlockSpec((slots, 4 * maps_count), lambda i: (0, 0)),
        ],
        out_specs=pl.BlockSpec((slots, 4 * maps_count), lambda i: (0, 0)),
        out_shape=jax.ShapeDtypeStruct((slots, 4 * maps_count), jnp.bfloat16),
        scratch_shapes=[pltpu.VMEM((2 * slots, 2 * maps_count), jnp.float32)],
        cost_estimate=pl.CostEstimate(
            flops=8 * slots * maps_count * pixel_slots,
            bytes_accessed=4 * maps_count * pixel_slots,
            transcendentals=0,
        ),
    )(rows, masked_weight, fine, coarse, live)


def operand_rows(wide, slot, cycles, stride):
    upper = wide[pl.ds(slot, cycles, stride=stride), :]
    quarter = upper.shape[1] // 4
    lower = jnp.concatenate(
        [
            upper[:, 3 * quarter :],
            -upper[:, 2 * quarter : 3 * quarter],
            -upper[:, quarter : 2 * quarter],
            upper[:, :quarter],
        ],
        axis=1,
    )
    return jnp.concatenate([upper, lower], axis=0)


def alm_kernel(stride, scalar_ref, gathered_ref, legendre_ref, out_ref, wide, operand):
    step = pl.program_id(0)
    height = out_ref.shape[0]
    columns = out_ref.shape[1]
    cycles = gathered_ref.shape[0] // stride

    @pl.when(step == 0)
    def _():
        wide[...] = gathered_ref[...].astype(jnp.float32)
        pair = scalar_ref[0]
        operand[...] = -jnp.concatenate(
            [
                operand_rows(wide, 2 * pair, cycles, stride),
                operand_rows(wide, 2 * pair + 1, cycles, stride),
            ],
            axis=1,
        )

    product = lax.dot_general(
        legendre_ref[...],
        operand[...].astype(jnp.bfloat16),
        (((0,), (0,)), ((), ())),
        preferred_element_type=jnp.float32,
    )
    row = step * height + lax.broadcasted_iota(jnp.int32, (height, columns), 0)
    out_ref[...] = jnp.where(row < scalar_ref[1], product[:, :columns], product[:, columns:])


def alm_call(scalars, gathered, stride, legendre_cols):
    inner, degree_count = legendre_cols.shape
    columns = gathered.shape[1]
    height = min(1024, degree_count)
    return pl.pallas_call(
        functools.partial(alm_kernel, stride),
        grid=(degree_count // height,),
        in_specs=[
            pl.BlockSpec(memory_space=pltpu.SMEM),
            pl.BlockSpec(gathered.shape, lambda i: (0, 0)),
            pl.BlockSpec((inner, height), lambda i: (0, i)),
        ],
        out_specs=pl.BlockSpec((height, columns), lambda i: (i, 0)),
        out_shape=jax.ShapeDtypeStruct((degree_count, columns), jnp.float32),
        scratch_shapes=[
            pltpu.VMEM(gathered.shape, jnp.float32),
            pltpu.VMEM((inner, 2 * columns), jnp.float32),
        ],
        cost_estimate=pl.CostEstimate(
            flops=4 * degree_count * inner * columns,
            bytes_accessed=4 * degree_count * columns,
            transcendentals=0,
        ),
    )(scalars, gathered, legendre_cols)


def spectra_kernel(stride, scale_ref, gathered_ref, legendre_ref, out_ref, wide, operands, dense, turned):
    step = pl.program_id(0)
    cycles = gathered_ref.shape[0] // stride
    inner = 2 * cycles
    slots = legendre_ref.shape[0] // inner
    height = legendre_ref.shape[1]
    per_group = 128 // inner
    group_count = slots // per_group

    @pl.when(step == 0)
    def _():
        wide[...] = gathered_ref[...].astype(jnp.float32)
        for slot in range(slots):
            operands[slot * inner : (slot + 1) * inner, :] = operand_rows(
                wide, slot, cycles, stride
            ).astype(jnp.bfloat16)

    def spread(tall, piece):
        parts = []
        for index in range(128 // piece):
            own = tall[index * piece : (index + 1) * piece]
            column = []
            if index > 0:
                column.append(jnp.zeros((index * piece, 128), tall.dtype))
            column.append(own)
            if (index + 1) * piece < 128:
                column.append(jnp.zeros((128 - (index + 1) * piece, 128), tall.dtype))
            parts.append(jnp.concatenate(column, axis=0))
        return jnp.concatenate(parts, axis=1)

    for group in range(group_count):
        wide_operand = spread(operands[group * 128 : (group + 1) * 128, :], inner)
        product = lax.dot_general(
            legendre_ref[group * 128 : (group + 1) * 128, :],
            wide_operand,
            (((0,), (0,)), ((), ())),
            preferred_element_type=jnp.float32,
        )
        for index in range(per_group):
            dense[pl.ds(group * per_group + index, height, stride=slots), :] = product[
                :, index * 128 : (index + 1) * 128
            ]

    per_batch = 128 // slots
    lane_group = lax.broadcasted_iota(jnp.int32, (8, 128), 1) // 32

    def batch(position, buffer):
        rows = dense[pl.ds(pl.multiple_of(position * 128, 128), 128), :]
        turned[buffer * 128 : (buffer + 1) * 128, :] = rows.T
        left = jnp.concatenate(
            [
                turned[pl.ds(buffer * 128 + 32 * part + quarter, 8, stride=4), :]
                for part in range(4)
                for quarter in range(4)
            ],
            axis=0,
        ).astype(jnp.bfloat16)
        gram = jnp.dot(
            left, spread(rows.astype(jnp.bfloat16), slots), preferred_element_type=jnp.float32
        )
        for index in range(per_batch):
            degree = position * per_batch + index
            factor = scale_ref[step * height + degree]
            for kind in range(2):
                result = None
                for turn in range(4):
                    first = 32 * (2 * kind) + 8 * ((2 * kind + turn) % 4)
                    second = 32 * (2 * kind + 1) + 8 * ((2 * kind + 1 + turn) % 4)
                    lanes = slice(index * 128, (index + 1) * 128)
                    value = jnp.where(
                        lane_group == 2 * kind,
                        gram[first : first + 8, lanes],
                        jnp.where(
                            lane_group == 2 * kind + 1, gram[second : second + 8, lanes], 0.0
                        ),
                    )
                    if turn > 0:
                        value = pltpu.roll(value, 32 * turn, axis=1)
                    result = value if result is None else result + value
                out_ref[pl.ds(degree * 16 + kind, 8, stride=2), :] = result * factor

    together = 8

    def several(position, carry):
        for buffer in range(together):
            batch(position * together + buffer, buffer)
        return carry

    lax.fori_loop(0, height // (per_batch * together), several, 0)


def spectra_call(scale, gathered, stride, legendre_rows):
    row_count, degree_local = legendre_rows.shape
    columns = gathered.shape[1]
    inner = 2 * (gathered.shape[0] // stride)
    slots = row_count // inner
    height = 128
    result = pl.pallas_call(
        functools.partial(spectra_kernel, stride),
        grid=(degree_local // height,),
        in_specs=[
            pl.BlockSpec(memory_space=pltpu.SMEM),
            pl.BlockSpec(gathered.shape, lambda i: (0, 0)),
            pl.BlockSpec((row_count, height), lambda i: (0, i)),
        ],
        out_specs=pl.BlockSpec((height * 16, 128), lambda i: (i, 0)),
        out_shape=jax.ShapeDtypeStruct((degree_local * 16, 128), jnp.float32),
        scratch_shapes=[
            pltpu.VMEM(gathered.shape, jnp.float32),
            pltpu.VMEM((row_count, columns), jnp.bfloat16),
            pltpu.VMEM((height * slots, columns), jnp.float32),
            pltpu.VMEM((1024, 128), jnp.float32),
        ],
        cost_estimate=pl.CostEstimate(
            flops=degree_local * slots * 4 * columns * columns,
            bytes_accessed=4 * degree_local * 2048,
            transcendentals=0,
        ),
    )(scale, gathered, legendre_rows)
    return (
        result.reshape(degree_local, 8, 2, 128)
        .transpose(0, 2, 1, 3)
        .reshape(degree_local, 2, 1024)
    )


def gather_kernel(devices, subs, payload_ref, out_ref, send_sem, recv_sem):
    me = lax.axis_index("band") * subs + lax.axis_index("sub")
    rows = payload_ref.shape[0]

    def place(index):
        return {"band": index // subs, "sub": index % subs}

    def slot(index):
        return out_ref.at[pl.ds(pl.multiple_of(index * rows, rows), rows), :]

    barrier = pltpu.get_barrier_semaphore()
    for offset in range(1, devices):
        pl.semaphore_signal(
            barrier,
            inc=1,
            device_id=place((me + offset) % devices),
            device_id_type=pl.DeviceIdType.MESH,
        )
    pl.semaphore_wait(barrier, devices - 1)

    def copy_of(offset, source):
        return pltpu.make_async_remote_copy(
            src_ref=payload_ref,
            dst_ref=slot(source),
            send_sem=send_sem.at[offset],
            recv_sem=recv_sem.at[offset],
            device_id=place((me + offset) % devices),
            device_id_type=pl.DeviceIdType.MESH,
        )

    for offset in range(1, devices):
        copy_of(offset, me).start()
    out_ref[pl.ds(pl.multiple_of(me * rows, rows), rows), :] = payload_ref[...]
    for offset in range(1, devices):
        copy_of(offset, (me + devices - offset) % devices).wait_recv()
    for offset in range(1, devices):
        copy_of(offset, me).wait_send()


def gather_call(payload, devices, subs):
    rows, columns = payload.shape
    return pl.pallas_call(
        functools.partial(gather_kernel, devices, subs),
        in_specs=[pl.BlockSpec(memory_space=pltpu.VMEM)],
        out_specs=pl.BlockSpec(memory_space=pltpu.VMEM),
        out_shape=jax.ShapeDtypeStruct((devices * rows, columns), payload.dtype),
        scratch_shapes=[
            pltpu.SemaphoreType.DMA((devices,)),
            pltpu.SemaphoreType.DMA((devices,)),
        ],
        compiler_params=pltpu.CompilerParams(collective_id=0, has_side_effects=True),
    )(payload)


def split_three(value):
    pieces = []
    rest = value
    for _ in range(3):
        piece = lax.reduce_precision(rest, 8, 7)
        pieces.append(piece)
        rest = rest - piece
    return pieces


def compact(sky_maps, sky_mask, pixel_counts, phi_offsets, low_orders, legendre):
    axes = ("band", "sub")
    devices = lax.axis_size(axes)
    device_index = lax.axis_index(axes)
    degree_count = legendre.shape[1]
    inner = legendre.shape[2]
    slots = 2 * low_orders.shape[0]
    orders = slot_orders(low_orders, degree_count)
    degree_local = degree_count // devices
    first_order = lax.dynamic_index_in_dim(low_orders, device_index, 0, keepdims=False)
    split_row = degree_count - first_order
    legendre_cols = legendre[0].T
    degrees = jnp.arange(degree_count, dtype=jnp.int32)[None, :]
    doubled = jnp.concatenate([legendre_cols, legendre_cols], axis=1)
    rolled = lax.dynamic_slice_in_dim(doubled, split_row, degree_count, 1)
    first = jnp.where(degrees >= first_order, rolled, 0.0).astype(jnp.bfloat16)
    second = jnp.where(degrees >= split_row, legendre_cols, 0.0).astype(jnp.bfloat16)
    sent = jnp.concatenate([first, second], axis=0)
    sent = sent.reshape(2 * inner, devices, degree_local).transpose(1, 0, 2)
    received = lax.all_to_all(sent, axes, split_axis=0, concat_axis=0, tiled=True)
    legendre_rows = received.reshape(slots * inner, degree_local)

    count = pixel_counts[0]
    valid = jnp.arange(sky_mask.shape[1], dtype=jnp.int32)[None, :] < count
    masked_weight = jnp.where(valid, sky_mask, 0.0)
    coefficients = fourier_call(sky_maps[0], masked_weight, count, phi_offsets[0], orders)
    square = split_three(jnp.sum(masked_weight * masked_weight))
    pixels = split_three(count.astype(jnp.float32))
    columns = coefficients.shape[1]
    extra = jnp.zeros((EXTRA, columns), jnp.float32)
    column_index = lax.broadcasted_iota(jnp.int32, (EXTRA, columns), 1)
    for index, piece in enumerate(square + pixels):
        extra = jnp.where(column_index == index, piece, extra)
    payload = jnp.concatenate([coefficients, extra.astype(jnp.bfloat16)], axis=0)
    gathered = gather_call(payload, devices, lax.axis_size("sub"))
    stride = slots + EXTRA
    pieces = gathered.reshape(devices, stride, columns)[:, slots, :6].astype(jnp.float32)
    weight = jnp.sum(pieces[:, :3]) / jnp.sum(pieces[:, 3:])
    scalars = jnp.stack([device_index.astype(jnp.int32), split_row])
    alm_packed = alm_call(scalars, gathered, stride, legendre_cols)
    own = device_index * degree_local + jnp.arange(degree_local, dtype=jnp.int32)
    counts = jnp.maximum(
        jnp.sum((orders[None, :] <= own[:, None]).astype(jnp.int32), axis=1), 1
    ).astype(jnp.float32)
    scale = 2.0 / (weight * counts)
    spectra = spectra_call(scale, gathered, stride, legendre_rows)
    return (alm_packed[None], spectra)


def general(sky_maps, sky_mask, pixel_counts, phi_offsets, low_orders, legendre):
    devices = lax.axis_size(("band", "sub"))
    device_index = lax.axis_index(("band", "sub"))
    degree_count = legendre.shape[1]
    orders = slot_orders(low_orders, degree_count)
    cycle_local = sky_maps.shape[0]
    maps_count = sky_maps.shape[2]
    pair_local = legendre.shape[0]
    slot_local = 2 * pair_local
    columns = 4 * maps_count
    valid_pixels = jnp.arange(sky_maps.shape[3], dtype=jnp.int32)[None, :] < pixel_counts[:, None]
    local_square = jnp.sum(jnp.where(valid_pixels, sky_mask * sky_mask, 0.0))
    local_pixels = jnp.sum(pixel_counts.astype(jnp.float32))
    total_square, total_pixels = lax.psum((local_square, local_pixels), ("band", "sub"))
    weight = total_square / total_pixels
    cycle_blocks = [
        cycle_fourier(sky_maps[0], sky_mask[0], pixel_counts[0], phi_offsets[0], orders)
    ]
    coefficients = jnp.stack(cycle_blocks, axis=1).reshape(
        devices, slot_local, cycle_local, columns
    )
    received = lax.all_to_all(
        coefficients, ("band", "sub"), split_axis=0, concat_axis=0, tiled=True
    )
    cycle_total = devices * cycle_local
    first_order = lax.dynamic_index_in_dim(
        low_orders, device_index * pair_local + 0, 0, keepdims=False
    )
    first_block = received[:, 0].reshape(cycle_total, columns)
    second_block = received[:, 1].reshape(cycle_total, columns)
    alm_pairs = [pair_alm(legendre[0], first_order, first_block, second_block)]
    alm_packed = jnp.stack(alm_pairs, axis=0)
    dense_local = dense_pair(alm_pairs[0], first_order)
    by_degree = lax.all_to_all(
        dense_local, ("band", "sub"), split_axis=1, concat_axis=0, tiled=True
    )
    degree_local = by_degree.shape[1]
    degrees = device_index * degree_local + jnp.arange(degree_local, dtype=jnp.int32)
    totals = outer_totals(by_degree, maps_count)
    spectra = scaled_spectra(totals, degrees, orders, weight, maps_count)
    return (alm_packed, spectra)


def local(sky_maps, sky_mask, pixel_counts, phi_offsets, low_orders, legendre):
    devices = lax.axis_size(("band", "sub"))
    fits = (
        sky_maps.shape[0] == 1
        and legendre.shape[0] == 1
        and sky_maps.shape[2] == 32
        and sky_maps.shape[3] % 2048 == 0
        and 2 * low_orders.shape[0] in (16, 32, 64)
        and legendre.shape[2] == 2 * devices
        and legendre.shape[2] in (16, 32, 64)
        and legendre.shape[1] % (128 * devices) == 0
        and legendre.shape[1] % 1024 == 0
    )
    body = compact if fits else general
    return body(sky_maps, sky_mask, pixel_counts, phi_offsets, low_orders, legendre)


def solution(mesh):
    placed = (
        P(("groups", "band", "sub"), None, None, None),
        P(("groups", "band", "sub"), None),
        P(("groups", "band", "sub")),
        P(("groups", "band", "sub")),
        P("groups"),
        P(("groups", "band", "sub"), None, None),
    )
    return jax.shard_map(
        local,
        mesh=mesh,
        in_specs=placed,
        out_specs=(
            P(("groups", "band", "sub"), None, None),
            P(("groups", "band", "sub"), None, None),
        ),
        check_vma=False,
    )
```
